32 devices in a mesh: loss: 4 (over x, core), tower: 4 (over z), pipe: 2 (over y).
Axes of the slice: x: 2, y: 2, z: 4, core: 2. Of those that a mesh axis runs over, the one named last changes fastest.
Arguments:
- image_feats: bfloat16 [4, 2, 24, 1536], P('loss', 'pipe', None, 'tower'), may hold values from -6 to 6
- text_tokens: bfloat16 [4, 2, 24, 64, 1152], P('loss', 'pipe', None, None, 'tower'), may hold values from -6 to 6
- lengths: int32 [4, 2, 24], P('loss', 'pipe'), may hold values from 1 to 64, as said below
- w_image: bfloat16 [1536, 1536], P('tower'), may hold values from -0.15625 to 0.15625
- w_text: bfloat16 [1152, 1536], P('tower'), may hold values from -0.1875 to 0.1875
- logit_scale: float32 [1], replicated, may hold values from 24 to 48
- logit_bias: float32 [1], replicated, may hold values from -4 to -2
Outputs:
- image_grad: float32 [4, 2, 24, 1536], P('loss', 'pipe', 'tower')
- text_grad: float32 [4, 2, 24, 1536], P('loss', 'pipe', 'tower')
The draws below stay inside these ranges and needn't reach their ends.
Inputs may be any that keep to these rules, and one draw needn't show every extreme that they name: `lengths`: in every group of 24 captions one caption has 64 tokens and one has a single token.
All inputs are finite; a program needn't handle non-finite values.
Results may differ from the reference program's by a relative error of at most 0.0036.
The reference program's roundings to bfloat16 on the way count: a program that leaves them out, or rounds other values in their place, can miss the bound.
Values may be sent and summed in bfloat16 or wider, within the bound.
A program may use at most 64 MiB of HBM per device.

```python
import math
import jax
import jax.numpy as jnp
from jax import lax

IMG_WIDTH = 1536
TEXT_WIDTH = 1152
EMB = 1536
TEXT_LEN = 64
GROUP = 24
N_LOSS = 4
N_PIPE = 2


def draw_lengths(key, part):
    values = jax.random.randint(key, (N_LOSS, N_PIPE, GROUP), 1, TEXT_LEN + 1, dtype=jnp.int32)
    values = values.at[:, :, 0].set(TEXT_LEN)
    return values.at[:, :, 1].set(1)


def levels(rng, dims, shards, low, top_value):
    level = 1.0
    for position, parts in shards:
        heights = jax.random.uniform(jax.random.fold_in(jax.random.fold_in(rng, 6), position), (parts,), jnp.float32, low / len(shards), top_value / len(shards))
        level = level * jnp.repeat(jnp.exp(heights), dims[position] // parts).reshape((-1,) + (1,) * (len(dims) - 1 - position))
    return level


def normal_values(key, shape, width, bound, shards=(), kind=jnp.bfloat16):
    gain = levels(key, shape, shards, -0.22, 0.18) if shards else 1.0
    drawn = jax.random.normal(key, shape, jnp.float32) * width * gain
    return jnp.minimum(jnp.maximum(drawn, -bound), bound).astype(kind)


def setup_inputs(seed: int = 0) -> dict:
    key_list = jax.random.split(jax.random.key(seed), 8)
    return {
        "image_feats": normal_values(key_list[0], (N_LOSS, N_PIPE, GROUP, IMG_WIDTH), 1.0, 6.0, ((0, 4), (1, 2), (3, 4))),
        "text_tokens": normal_values(key_list[1], (N_LOSS, N_PIPE, GROUP, TEXT_LEN, TEXT_WIDTH), 1.0, 6.0, ((0, 4), (1, 2), (4, 4))),
        "lengths": draw_lengths(jax.random.fold_in(key_list[7], 71), 0),
        "w_image": normal_values(key_list[3], (IMG_WIDTH, EMB), IMG_WIDTH ** -0.5, 0.15625, ((0, 4),)),
        "w_text": normal_values(key_list[4], (TEXT_WIDTH, EMB), TEXT_WIDTH ** -0.5, 0.1875, ((0, 4),)),
        "logit_scale": jnp.clip(jnp.exp(jax.random.uniform(key_list[5], (1,), jnp.float32, math.log(24.0), math.log(48.0))), 24.0, 48.0),
        "logit_bias": jnp.clip(jax.random.uniform(key_list[6], (1,), jnp.float32, -4.0, -2.0), -4.0, -2.0),
    }


def normalize(raw):
    return raw * lax.rsqrt(lax.optimization_barrier(jnp.sum(raw * raw, axis=-1, keepdims=True)) + 1e-06)

def reference(image_feats, text_tokens, lengths, w_image, w_text, logit_scale, logit_bias):
    batch = N_LOSS * N_PIPE * GROUP
    images = image_feats.reshape(batch, IMG_WIDTH)
    image_unit = normalize(jnp.dot(images, w_image, preferred_element_type=jnp.float32)).astype(jnp.bfloat16)
    places = jnp.arange(TEXT_LEN, dtype=jnp.int32)[None, :]

    def pool(block):
        words, counts = block
        keep = (places < counts[:, None]).astype(jnp.float32)
        summed = jnp.einsum('bl,bld->bd', keep, words.astype(jnp.float32))
        return (summed / counts.astype(jnp.float32)[:, None]).astype(jnp.bfloat16)
    pooled = lax.map(pool, (text_tokens.reshape(batch // GROUP, GROUP, TEXT_LEN, TEXT_WIDTH), lengths.reshape(batch // GROUP, GROUP))).reshape(batch, TEXT_WIDTH)
    text_unit = normalize(jnp.dot(pooled, w_text, preferred_element_type=jnp.float32)).astype(jnp.bfloat16)
    scale = logit_scale[0]
    shift = logit_bias[0]
    text_ids = jnp.arange(batch, dtype=jnp.int32)

    def step(carry, block):
        rows, row_ids = block
        scores = jnp.dot(rows, text_unit.T, preferred_element_type=jnp.float32)
        match = (row_ids[:, None] == text_ids[None, :]).astype(jnp.float32)
        grads = (jax.nn.sigmoid(scale * scores + shift) - match).astype(jnp.bfloat16)
        image_part = scale * jnp.dot(grads, text_unit, preferred_element_type=jnp.float32)
        carry = carry + scale * jnp.dot(grads.T, rows, preferred_element_type=jnp.float32)
        return (carry, image_part)
    start = jnp.zeros((batch, EMB), jnp.float32)
    text_grad, image_parts = lax.scan(step, start, (image_unit.reshape(batch // GROUP, GROUP, EMB), text_ids.reshape(batch // GROUP, GROUP)))
    image_grad = image_parts.reshape(N_LOSS, N_PIPE, GROUP, EMB)
    return (image_grad, text_grad.reshape(N_LOSS, N_PIPE, GROUP, EMB))
```

```python
import functools

import jax
import jax.numpy as jnp
from jax import lax
from jax.experimental import pallas as pl
from jax.experimental.pallas import tpu as pltpu
from jax.sharding import PartitionSpec as P

MESH = pl.DeviceIdType.MESH
WIRE = jnp.bfloat16
CODE = jnp.int16
F32 = jnp.float32
BF16 = jnp.bfloat16
UNROLL = 16
LANES = 128
STEPS = 32752.0
LN2 = 0.6931471805599453


def each(lo, hi, body):
    if hi - lo <= UNROLL:
        for k in reversed(range(lo, hi)):
            body(k)
    else:
        lax.fori_loop(lo, hi, lambda k, c: (body(k), c)[1], 0)


def partner(me, k, n):
    if n <= UNROLL and n & (n - 1) == 0:
        q = me
        for b in range(n.bit_length() - 1):
            if (k >> b) & 1:
                q = q + (1 - 2 * lax.rem(me // (1 << b), 2)) * (1 << b)
        return q, q
    return lax.rem(me + k, n), lax.rem(me + n - k, n)


def kernel(
    sub, towers, pipes, planes,
    scale_hbm, shift_hbm, feats_hbm, words_hbm, lens_hbm, wi_hbm, wt_hbm,
    image_out, text_out,
    scale_ref, shift_ref, feats, words, lens, wi, wt,
    flat_i, flat_t, power_i, power_t, part_i, part_t, got_i, got_t, code,
    full_i, full_t, images, texts, sums_i, sums_t, term_i, term_t, back_i, back_t,
    load_sem, s1, r1, s2, r2, s3, r3, s4, r4, s5, r5, s6, r6,
):
    group, width = feats.shape
    length = words.shape[1]
    emb = wi.shape[1]
    chunks = emb // LANES
    rows = sub * chunks
    span = term_i.shape[1]
    tower = lax.axis_index("tower")
    plane = lax.axis_index("loss") * pipes + lax.axis_index("pipe")

    def tower_at(k):
        return {"tower": partner(tower, k, towers)[0]}

    def plane_at(k):
        q = partner(plane, k, planes)[0]
        return {"loss": q // pipes, "pipe": lax.rem(q, pipes)}

    def block(i):
        at = i * rows
        return pl.multiple_of(at, 8) if rows % 8 == 0 else at

    loads = []
    for n, (src, dst) in enumerate((
        (feats_hbm.at[0, 0], feats),
        (wi_hbm, wi),
        (lens_hbm.at[0], lens),
        (words_hbm.at[0, 0], words),
        (wt_hbm, wt),
        (scale_hbm, scale_ref),
        (shift_hbm, shift_ref),
    )):
        loads.append(pltpu.make_async_copy(src, dst, load_sem.at[n]))
        loads[-1].start()

    barrier = pltpu.get_barrier_semaphore()
    each(1, towers, lambda k: pl.semaphore_signal(
        barrier, inc=1, device_id=tower_at(k), device_id_type=MESH))
    each(1, planes, lambda k: pl.semaphore_signal(
        barrier, inc=1, device_id=plane_at(k), device_id_type=MESH))

    def spread(ref, start, x):
        for c in range(chunks):
            ref[pl.ds(start + c, x.shape[0], stride=chunks), :] = x[:, c * LANES:(c + 1) * LANES]

    def gather(ref, start, n):
        return jnp.concatenate(
            [ref[pl.ds(start + c, n, stride=chunks), :] for c in range(chunks)], axis=1)

    def up(power):
        return jnp.exp(power * -LN2) * STEPS

    def down(power):
        return jnp.exp(power * LN2) * (1.0 / STEPS)

    def encode(raw, flat, power_ref, part):
        most = jnp.max(jnp.abs(raw), axis=1, keepdims=True)
        power = jnp.floor(jnp.log(jnp.maximum(most, 1e-30)) * (1.0 / LN2)) + 1.0
        spread(flat, 0, raw * up(power))
        power_ref[0:group, :] = jnp.broadcast_to(power, (group, LANES))
        for d in range(towers):
            values = jnp.round(flat[d * rows:(d + 1) * rows, :])
            part[d, 0:rows, :] = values.astype(jnp.int32).astype(CODE)
            part[d, span:span + sub, :] = power_ref[
                d * sub:(d + 1) * sub, :].astype(jnp.int32).astype(CODE)

    def scatter(k, part, got, send, recv):
        return pltpu.make_async_remote_copy(
            src_ref=part.at[partner(tower, k, towers)[0]], dst_ref=got.at[k - 1],
            send_sem=send.at[k - 1], recv_sem=recv.at[k - 1],
            device_id=tower_at(k), device_id_type=MESH)

    loads[0].wait()
    loads[1].wait()
    encode(jnp.dot(feats[...], wi[...], preferred_element_type=F32), flat_i, power_i, part_i)
    pl.semaphore_wait(barrier, towers + planes - 2)
    each(1, towers, lambda k: scatter(k, part_i, got_i, s2, r2).start())

    loads[2].wait()
    diagonal = (lax.broadcasted_iota(jnp.int32, (group, group), 0)
                == lax.broadcasted_iota(jnp.int32, (group, group), 1))
    counts = jnp.sum(jnp.where(diagonal, lens[...].astype(F32), 0.0), axis=1, keepdims=True)
    spot = lax.broadcasted_iota(jnp.int32, (group, group * length), 1)
    first = lax.broadcasted_iota(jnp.int32, (group, group * length), 0) * length
    keep = (spot >= first) & (spot < first + counts.astype(jnp.int32))
    keep = jnp.where(keep, 1.0, 0.0).astype(BF16)
    loads[3].wait()
    summed = jnp.dot(keep, words[...].reshape(group * length, words.shape[2]),
                     preferred_element_type=F32)
    pooled = (summed / counts).astype(BF16)
    loads[4].wait()
    encode(jnp.dot(pooled, wt[...], preferred_element_type=F32), flat_t, power_t, part_t)
    each(1, towers, lambda k: scatter(k, part_t, got_t, s1, r1).start())

    def unit(flat, power_ref, part, got, send, recv):
        raw = gather(flat, block(tower), sub) * down(power_ref[pl.ds(tower * sub, sub), 0:1])
        for k in reversed(range(1, towers)):
            scatter(k, part, got, send, recv).wait_recv()
            code[...] = got[k - 1, 0:rows, :].astype(jnp.int32).astype(F32)
            power = got[k - 1, span:span + sub, :].astype(jnp.int32).astype(F32)[:, 0:1]
            raw = raw + gather(code, 0, sub) * down(power)
        size = jnp.sum(raw * raw, axis=-1, keepdims=True) + 1e-06
        return raw * lax.rsqrt(size)

    def give_t(k):
        return pltpu.make_async_remote_copy(
            src_ref=texts.at[plane], dst_ref=texts.at[plane],
            send_sem=s3.at[k - 1], recv_sem=r3.at[k - 1],
            device_id=plane_at(k), device_id_type=MESH)

    def give_i(k):
        return pltpu.make_async_remote_copy(
            src_ref=images.at[tower], dst_ref=images.at[tower],
            send_sem=s4.at[k - 1], recv_sem=r4.at[k - 1],
            device_id=tower_at(k), device_id_type=MESH)

    spread(full_i, block(tower), unit(flat_i, power_i, part_i, got_i, s2, r2))
    images[tower, 0:rows, :] = full_i[pl.ds(block(tower), rows), :].astype(BF16)
    each(1, towers, lambda k: give_i(k).start())
    spread(full_t, block(plane), unit(flat_t, power_t, part_t, got_t, s1, r1))
    texts[plane, 0:rows, :] = full_t[pl.ds(block(plane), rows), :].astype(BF16)
    each(1, planes, lambda k: give_t(k).start())

    def take_i(k):
        give_i(k).wait_recv()
        q = partner(tower, k, towers)[1]
        full_i[pl.ds(block(q), rows), :] = images[q, 0:rows, :].astype(F32)

    def take_t(k):
        give_t(k).wait_recv()
        q = partner(plane, k, planes)[1]
        full_t[pl.ds(block(q), rows), :] = texts[q, 0:rows, :].astype(F32)

    loads[5].wait()
    loads[6].wait()
    scale = scale_ref[0]
    shift = shift_ref[0]
    cols = planes * sub
    each(1, towers, take_i)
    all_i = gather(full_i, 0, group).astype(BF16)
    each(1, planes, take_t)
    all_t = gather(full_t, 0, cols).astype(BF16)
    scores = lax.dot_general(all_i, all_t, (((1,), (1,)), ((), ())), preferred_element_type=F32)
    at_i = lax.broadcasted_iota(jnp.int32, (group, cols), 0) - tower * sub
    at_t = lax.broadcasted_iota(jnp.int32, (group, cols), 1) - plane * sub
    match = jnp.where((at_i == at_t) & (at_i >= 0) & (at_i < sub), 1.0, 0.0)
    grads = jax.nn.sigmoid(scale * scores + shift) - match

    def back_image(k):
        return pltpu.make_async_remote_copy(
            src_ref=term_i.at[partner(tower, k, towers)[0]], dst_ref=back_i.at[k - 1],
            send_sem=s5.at[k - 1], recv_sem=r5.at[k - 1],
            device_id=tower_at(k), device_id_type=MESH)

    def back_text(k):
        return pltpu.make_async_remote_copy(
            src_ref=term_t.at[partner(plane, k, planes)[0]], dst_ref=back_t.at[k - 1],
            send_sem=s6.at[k - 1], recv_sem=r6.at[k - 1],
            device_id=plane_at(k), device_id_type=MESH)

    def stage(n, sums, term):
        for d in range(n):
            term[d, 0:rows, :] = sums[d * rows:(d + 1) * rows, :].astype(WIRE)

    spread(sums_i, 0, jnp.dot(grads.astype(BF16), all_t, preferred_element_type=F32))
    stage(towers, sums_i, term_i)
    each(1, towers, lambda k: back_image(k).start())
    spread(sums_t, 0, jnp.dot(grads.T.astype(BF16), all_i, preferred_element_type=F32))
    stage(planes, sums_t, term_t)
    each(1, planes, lambda k: back_text(k).start())

    def total(sums, me, back, wait, n, out):
        each(1, n, wait)
        value = sums[pl.ds(block(me), rows), :]
        value = scale * (value + jnp.sum(back[:, 0:rows, :].astype(F32), axis=0))
        code[...] = value
        out[:, 0, :] = gather(code, 0, sub)

    total(sums_t, plane, back_t, lambda k: back_text(k).wait_recv(), planes, text_out)
    total(sums_i, tower, back_i, lambda k: back_image(k).wait_recv(), towers, image_out)

    each(1, towers, lambda k: scatter(k, part_t, got_t, s1, r1).wait_send())
    each(1, towers, lambda k: scatter(k, part_i, got_i, s2, r2).wait_send())
    each(1, planes, lambda k: give_t(k).wait_send())
    each(1, towers, lambda k: give_i(k).wait_send())
    each(1, towers, lambda k: back_image(k).wait_send())
    each(1, planes, lambda k: back_text(k).wait_send())


def finish(image_ref, text_ref, image_out, text_out):
    image_out[...] = image_ref[...]
    text_out[...] = text_ref[...]


def up_to(n, m):
    return -(-n // m) * m


def per_device(towers, pipes, planes, image_feats, text_tokens, lengths, w_image, w_text,
               logit_scale, logit_bias):
    group = image_feats.shape[2]
    emb = w_image.shape[1]
    sub = group // towers
    rows = sub * emb // LANES
    span = up_to(rows, 8)
    note = up_to(span + sub, 16)
    out = jax.ShapeDtypeStruct((sub, 1, emb), F32)
    sems = []
    for n in (towers, towers, planes, towers, towers, planes):
        sems += [pltpu.SemaphoreType.DMA((n - 1,))] * 2
    outs = pl.pallas_call(
        functools.partial(kernel, sub, towers, pipes, planes),
        out_shape=(out, out),
        in_specs=[pl.BlockSpec(memory_space=pl.ANY)] * 7,
        out_specs=(pl.BlockSpec(memory_space=pltpu.VMEM),) * 2,
        scratch_shapes=[
            pltpu.SMEM(logit_scale.shape, F32),
            pltpu.SMEM(logit_bias.shape, F32),
            pltpu.VMEM(image_feats.shape[2:], image_feats.dtype),
            pltpu.VMEM(text_tokens.shape[2:], text_tokens.dtype),
            pltpu.VMEM(lengths.shape[1:], lengths.dtype),
            pltpu.VMEM(w_image.shape, w_image.dtype),
            pltpu.VMEM(w_text.shape, w_text.dtype),
            pltpu.VMEM((towers * rows, LANES), F32),
            pltpu.VMEM((towers * rows, LANES), F32),
            pltpu.VMEM((up_to(group, 8), LANES), F32),
            pltpu.VMEM((up_to(group, 8), LANES), F32),
            pltpu.VMEM((towers, note, LANES), CODE),
            pltpu.VMEM((towers, note, LANES), CODE),
            pltpu.VMEM((towers - 1, note, LANES), CODE),
            pltpu.VMEM((towers - 1, note, LANES), CODE),
            pltpu.VMEM((rows, LANES), F32),
            pltpu.VMEM((towers * rows, LANES), F32),
            pltpu.VMEM((planes * rows, LANES), F32),
            pltpu.VMEM((towers, span, LANES), BF16),
            pltpu.VMEM((planes, span, LANES), BF16),
            pltpu.VMEM((towers * rows, LANES), F32),
            pltpu.VMEM((planes * rows, LANES), F32),
            pltpu.VMEM((towers, span, LANES), WIRE),
            pltpu.VMEM((planes, span, LANES), WIRE),
            pltpu.VMEM((towers - 1, span, LANES), WIRE),
            pltpu.VMEM((planes - 1, span, LANES), WIRE),
            pltpu.SemaphoreType.DMA((7,)),
        ] + sems,
        compiler_params=pltpu.CompilerParams(collective_id=0, has_side_effects=True),
    )(logit_scale, logit_bias, image_feats, text_tokens, lengths, w_image, w_text)
    outs = pl.pallas_call(
        finish,
        out_shape=(out, out),
        in_specs=[pl.BlockSpec(memory_space=pltpu.VMEM)] * 2,
        out_specs=(pl.BlockSpec(memory_space=pltpu.VMEM),) * 2,
    )(*outs)
    return tuple(o.reshape(1, 1, sub, emb) for o in outs)


def solution(mesh):
    shape = dict(mesh.shape)
    planes = shape["loss"] * shape["pipe"]
    return jax.shard_map(
        functools.partial(per_device, shape["tower"], shape["pipe"], planes),
        mesh=mesh,
        in_specs=(
            P("loss", "pipe", None, "tower"),
            P("loss", "pipe", None, None, "tower"),
            P("loss", "pipe", None),
            P("tower", None),
            P("tower", None),
            P(),
            P(),
        ),
        out_specs=(P("loss", "pipe", "tower", None), P("loss", "pipe", "tower", None)),
        check_vma=False,
    )
```

```python
import functools

import jax
import jax.numpy as jnp
from jax import lax
from jax.experimental import pallas as pl
from jax.experimental.pallas import tpu as pltpu
from jax.sharding import PartitionSpec as P

MESH = pl.DeviceIdType.MESH
WIRE = jnp.bfloat16
CODE = jnp.int16
F32 = jnp.float32
BF16 = jnp.bfloat16
UNROLL = 16
LANES = 128
STEPS = 32752.0
LN2 = 0.6931471805599453


def each(lo, hi, body):
    if hi - lo <= UNROLL:
        for k in reversed(range(lo, hi)):
            body(k)
    else:
        lax.fori_loop(lo, hi, lambda k, c: (body(k), c)[1], 0)


def partner(me, k, n):
    if n <= UNROLL and n & (n - 1) == 0:
        q = me
        for b in range(n.bit_length() - 1):
            if (k >> b) & 1:
                q = q + (1 - 2 * lax.rem(me // (1 << b), 2)) * (1 << b)
        return q, q
    return lax.rem(me + k, n), lax.rem(me + n - k, n)


def kernel(
    sub, towers, pipes, planes,
    scale_hbm, shift_hbm, feats_hbm, words_hbm, lens_hbm, wi_hbm, wt_hbm,
    image_out, text_out,
    scale_ref, shift_ref, feats, words, lens, wi, wt,
    flat_i, flat_t, power_i, power_t, part_i, part_t, got_i, got_t, code,
    full_i, full_t, images, texts, sums_i, sums_t, term_i, term_t, back_i, back_t,
    load_sem, s1, r1, s2, r2, s3, r3, s4, r4, s5, r5, s6, r6,
):
    group, width = feats.shape
    length = words.shape[1]
    emb = wi.shape[1]
    chunks = emb // LANES
    rows = sub * chunks
    span = term_i.shape[1]
    tower = lax.axis_index("tower")
    plane = lax.axis_index("loss") * pipes + lax.axis_index("pipe")

    def tower_at(k):
        return {"tower": partner(tower, k, towers)[0]}

    def plane_at(k):
        q = partner(plane, k, planes)[0]
        return {"loss": q // pipes, "pipe": lax.rem(q, pipes)}

    def block(i):
        at = i * rows
        return pl.multiple_of(at, 8) if rows % 8 == 0 else at

    loads = []
    for n, (src, dst) in enumerate((
        (feats_hbm.at[0, 0], feats),
        (wi_hbm, wi),
        (lens_hbm.at[0], lens),
        (words_hbm.at[0, 0], words),
        (wt_hbm, wt),
        (scale_hbm, scale_ref),
        (shift_hbm, shift_ref),
    )):
        loads.append(pltpu.make_async_copy(src, dst, load_sem.at[n]))
        loads[-1].start()

    barrier = pltpu.get_barrier_semaphore()
    each(1, towers, lambda k: pl.semaphore_signal(
        barrier, inc=1, device_id=tower_at(k), device_id_type=MESH))
    each(1, planes, lambda k: pl.semaphore_signal(
        barrier, inc=1, device_id=plane_at(k), device_id_type=MESH))

    def spread(ref, start, x):
        for c in range(chunks):
            ref[pl.ds(start + c, x.shape[0], stride=chunks), :] = x[:, c * LANES:(c + 1) * LANES]

    def gather(ref, start, n):
        return jnp.concatenate(
            [ref[pl.ds(start + c, n, stride=chunks), :] for c in range(chunks)], axis=1)

    def up(power):
        return jnp.exp(power * -LN2) * STEPS

    def down(power):
        return jnp.exp(power * LN2) * (1.0 / STEPS)

    def encode(raw, flat, power_ref, part):
        most = jnp.max(jnp.abs(raw), axis=1, keepdims=True)
        power = jnp.floor(jnp.log(jnp.maximum(most, 1e-30)) * (1.0 / LN2)) + 1.0
        spread(flat, 0, raw * up(power))
        power_ref[0:group, :] = jnp.broadcast_to(power, (group, LANES))
        for d in range(towers):
            values = jnp.round(flat[d * rows:(d + 1) * rows, :])
            part[d, 0:rows, :] = values.astype(jnp.int32).astype(CODE)
            part[d, span:span + sub, :] = power_ref[
                d * sub:(d + 1) * sub, :].astype(jnp.int32).astype(CODE)

    def scatter(k, part, got, send, recv):
        return pltpu.make_async_remote_copy(
            src_ref=part.at[partner(tower, k, towers)[0]], dst_ref=got.at[k - 1],
            send_sem=send.at[k - 1], recv_sem=recv.at[k - 1],
            device_id=tower_at(k), device_id_type=MESH)

    loads[0].wait()
    loads[1].wait()
    encode(jnp.dot(feats[...], wi[...], preferred_element_type=F32), flat_i, power_i, part_i)
    pl.semaphore_wait(barrier, towers + planes - 2)
    each(1, towers, lambda k: scatter(k, part_i, got_i, s2, r2).start())

    loads[2].wait()
    diagonal = (lax.broadcasted_iota(jnp.int32, (group, group), 0)
                == lax.broadcasted_iota(jnp.int32, (group, group), 1))
    counts = jnp.sum(jnp.where(diagonal, lens[...].astype(F32), 0.0), axis=1, keepdims=True)
    spot = lax.broadcasted_iota(jnp.int32, (group, group * length), 1)
    first = lax.broadcasted_iota(jnp.int32, (group, group * length), 0) * length
    keep = (spot >= first) & (spot < first + counts.astype(jnp.int32))
    keep = jnp.where(keep, 1.0, 0.0).astype(BF16)
    loads[3].wait()
    summed = jnp.dot(keep, words[...].reshape(group * length, words.shape[2]),
                     preferred_element_type=F32)
    pooled = (summed / counts).astype(BF16)
    loads[4].wait()
    encode(jnp.dot(pooled, wt[...], preferred_element_type=F32), flat_t, power_t, part_t)
    each(1, towers, lambda k: scatter(k, part_t, got_t, s1, r1).start())

    def unit(flat, power_ref, part, got, send, recv):
        raw = gather(flat, block(tower), sub) * down(power_ref[pl.ds(tower * sub, sub), 0:1])
        for k in reversed(range(1, towers)):
            scatter(k, part, got, send, recv).wait_recv()
            code[...] = got[k - 1, 0:rows, :].astype(jnp.int32).astype(F32)
            power = got[k - 1, span:span + sub, :].astype(jnp.int32).astype(F32)[:, 0:1]
            raw = raw + gather(code, 0, sub) * down(power)
        size = jnp.sum(raw * raw, axis=-1, keepdims=True) + 1e-06
        return raw * lax.rsqrt(size)

    def give_t(k):
        return pltpu.make_async_remote_copy(
            src_ref=texts.at[plane], dst_ref=texts.at[plane],
            send_sem=s3.at[k - 1], recv_sem=r3.at[k - 1],
            device_id=plane_at(k), device_id_type=MESH)

    def give_i(k):
        return pltpu.make_async_remote_copy(
            src_ref=images.at[tower], dst_ref=images.at[tower],
            send_sem=s4.at[k - 1], recv_sem=r4.at[k - 1],
            device_id=tower_at(k), device_id_type=MESH)

    spread(full_i, block(tower), unit(flat_i, power_i, part_i, got_i, s2, r2))
    images[tower, 0:rows, :] = full_i[pl.ds(block(tower), rows), :].astype(BF16)
    each(1, towers, lambda k: give_i(k).start())
    spread(full_t, block(plane), unit(flat_t, power_t, part_t, got_t, s1, r1))
    texts[plane, 0:rows, :] = full_t[pl.ds(block(plane), rows), :].astype(BF16)
    each(1, planes, lambda k: give_t(k).start())

    def take_i(k):
        give_i(k).wait_recv()
        q = partner(tower, k, towers)[1]
        full_i[pl.ds(block(q), rows), :] = images[q, 0:rows, :].astype(F32)

    def take_t(k):
        give_t(k).wait_recv()
        q = partner(plane, k, planes)[1]
        full_t[pl.ds(block(q), rows), :] = texts[q, 0:rows, :].astype(F32)

    loads[5].wait()
    loads[6].wait()
    scale = scale_ref[0]
    shift = shift_ref[0]
    cols = planes * sub
    each(1, towers, take_i)
    all_i = gather(full_i, 0, group).astype(BF16)
    each(1, planes, take_t)
    all_t = gather(full_t, 0, cols).astype(BF16)
    scores = lax.dot_general(all_i, all_t, (((1,), (1,)), ((), ())), preferred_element_type=F32)
    at_i = lax.broadcasted_iota(jnp.int32, (group, cols), 0) - tower * sub
    at_t = lax.broadcasted_iota(jnp.int32, (group, cols), 1) - plane * sub
    match = jnp.where((at_i == at_t) & (at_i >= 0) & (at_i < sub), 1.0, 0.0)
    grads = jax.nn.sigmoid(scale * scores + shift) - match

    def back_image(k):
        return pltpu.make_async_remote_copy(
            src_ref=term_i.at[partner(tower, k, towers)[0]], dst_ref=back_i.at[k - 1],
            send_sem=s5.at[k - 1], recv_sem=r5.at[k - 1],
            device_id=tower_at(k), device_id_type=MESH)

    def back_text(k):
        return pltpu.make_async_remote_copy(
            src_ref=term_t.at[partner(plane, k, planes)[0]], dst_ref=back_t.at[k - 1],
            send_sem=s6.at[k - 1], recv_sem=r6.at[k - 1],
            device_id=plane_at(k), device_id_type=MESH)

    def stage(n, sums, term):
        for d in range(n):
            term[d, 0:rows, :] = sums[d * rows:(d + 1) * rows, :].astype(WIRE)

    spread(sums_i, 0, jnp.dot(grads.astype(BF16), all_t, preferred_element_type=F32))
    stage(towers, sums_i, term_i)
    each(1, towers, lambda k: back_image(k).start())
    spread(sums_t, 0, jnp.dot(grads.T.astype(BF16), all_i, preferred_element_type=F32))
    stage(planes, sums_t, term_t)
    each(1, planes, lambda k: back_text(k).start())

    def total(sums, me, back, wait, n, out):
        each(1, n, wait)
        value = sums[pl.ds(block(me), rows), :]
        value = scale * (value + jnp.sum(back[:, 0:rows, :].astype(F32), axis=0))
        code[...] = value
        out[:, 0, :] = gather(code, 0, sub)

    total(sums_t, plane, back_t, lambda k: back_text(k).wait_recv(), planes, text_out)
    total(sums_i, tower, back_i, lambda k: back_image(k).wait_recv(), towers, image_out)

    each(1, towers, lambda k: scatter(k, part_t, got_t, s1, r1).wait_send())
    each(1, towers, lambda k: scatter(k, part_i, got_i, s2, r2).wait_send())
    each(1, planes, lambda k: give_t(k).wait_send())
    each(1, towers, lambda k: give_i(k).wait_send())
    each(1, towers, lambda k: back_image(k).wait_send())
    each(1, planes, lambda k: back_text(k).wait_send())


def finish(image_ref, text_ref, image_out, text_out):
    image_out[...] = image_ref[...]
    text_out[...] = text_ref[...]


def up_to(n, m):
    return -(-n // m) * m


def per_device(towers, pipes, planes, image_feats, text_tokens, lengths, w_image, w_text,
               logit_scale, logit_bias):
    group = image_feats.shape[2]
    emb = w_image.shape[1]
    sub = group // towers
    rows = sub * emb // LANES
    span = up_to(rows, 8)
    note = up_to(span + sub, 16)
    out = jax.ShapeDtypeStruct((sub, 1, emb), F32)
    sems = []
    for n in (towers, towers, planes, towers, towers, planes):
        sems += [pltpu.SemaphoreType.DMA((n - 1,))] * 2
    arrays = [pltpu.with_memory_space_constraint(x, pltpu.HBM) for x in (
        image_feats, text_tokens, lengths, w_image, w_text)]
    outs = pl.pallas_call(
        functools.partial(kernel, sub, towers, pipes, planes),
        out_shape=(out, out),
        in_specs=[pl.BlockSpec(memory_space=pl.ANY)] * 7,
        out_specs=(pl.BlockSpec(memory_space=pltpu.VMEM),) * 2,
        scratch_shapes=[
            pltpu.SMEM(logit_scale.shape, F32),
            pltpu.SMEM(logit_bias.shape, F32),
            pltpu.VMEM(image_feats.shape[2:], image_feats.dtype),
            pltpu.VMEM(text_tokens.shape[2:], text_tokens.dtype),
            pltpu.VMEM(lengths.shape[1:], lengths.dtype),
            pltpu.VMEM(w_image.shape, w_image.dtype),
            pltpu.VMEM(w_text.shape, w_text.dtype),
            pltpu.VMEM((towers * rows, LANES), F32),
            pltpu.VMEM((towers * rows, LANES), F32),
            pltpu.VMEM((up_to(group, 8), LANES), F32),
            pltpu.VMEM((up_to(group, 8), LANES), F32),
            pltpu.VMEM((towers, note, LANES), CODE),
            pltpu.VMEM((towers, note, LANES), CODE),
            pltpu.VMEM((towers - 1, note, LANES), CODE),
            pltpu.VMEM((towers - 1, note, LANES), CODE),
            pltpu.VMEM((rows, LANES), F32),
            pltpu.VMEM((towers * rows, LANES), F32),
            pltpu.VMEM((planes * rows, LANES), F32),
            pltpu.VMEM((towers, span, LANES), BF16),
            pltpu.VMEM((planes, span, LANES), BF16),
            pltpu.VMEM((towers * rows, LANES), F32),
            pltpu.VMEM((planes * rows, LANES), F32),
            pltpu.VMEM((towers, span, LANES), WIRE),
            pltpu.VMEM((planes, span, LANES), WIRE),
            pltpu.VMEM((towers - 1, span, LANES), WIRE),
            pltpu.VMEM((planes - 1, span, LANES), WIRE),
            pltpu.SemaphoreType.DMA((7,)),
        ] + sems,
        compiler_params=pltpu.CompilerParams(
            collective_id=0, has_side_effects=True, vmem_limit_bytes=24 * 2**20),
    )(logit_scale, logit_bias, *arrays)
    outs = pl.pallas_call(
        finish,
        out_shape=(out, out),
        in_specs=[pl.BlockSpec(memory_space=pltpu.VMEM)] * 2,
        out_specs=(pl.BlockSpec(memory_space=pltpu.VMEM),) * 2,
        compiler_params=pltpu.CompilerParams(vmem_limit_bytes=2**20),
    )(*outs)
    return tuple(o.reshape(1, 1, sub, emb) for o in outs)


def solution(mesh):
    shape = dict(mesh.shape)
    planes = shape["loss"] * shape["pipe"]
    return jax.shard_map(
        functools.partial(per_device, shape["tower"], shape["pipe"], planes),
        mesh=mesh,
        in_specs=(
            P("loss", "pipe", None, "tower"),
            P("loss", "pipe", None, None, "tower"),
            P("loss", "pipe", None),
            P("tower", None),
            P("tower", None),
            P(),
            P(),
        ),
        out_specs=(P("loss", "pipe", "tower", None), P("loss", "pipe", "tower", None)),
        check_vma=False,
    )
```

```python
import functools

import jax
import jax.numpy as jnp
from jax import lax
from jax.experimental import pallas as pl
from jax.experimental.pallas import tpu as pltpu
from jax.sharding import PartitionSpec as P

MESH = pl.DeviceIdType.MESH
WIRE = jnp.bfloat16
CODE = jnp.int16
F32 = jnp.float32
BF16 = jnp.bfloat16
UNROLL = 16
LANES = 128
STEPS = 32752.0
LN2 = 0.6931471805599453


def each(lo, hi, body):
    if hi - lo <= UNROLL:
        for k in reversed(range(lo, hi)):
            body(k)
    else:
        lax.fori_loop(lo, hi, lambda k, c: (body(k), c)[1], 0)


def near(lo, hi, body):
    if hi - lo <= UNROLL:
        for k in sorted(range(lo, hi), key=lambda k: (bin(k).count("1"), k)):
            body(k)
    else:
        each(lo, hi, body)


def partner(me, k, n):
    if n <= UNROLL and n & (n - 1) == 0:
        q = me
        for b in range(n.bit_length() - 1):
            if (k >> b) & 1:
                q = q + (1 - 2 * lax.rem(me // (1 << b), 2)) * (1 << b)
        return q, q
    return lax.rem(me + k, n), lax.rem(me + n - k, n)


def kernel(
    sub, towers, pipes, planes,
    scale_hbm, shift_hbm, feats_hbm, words_hbm, lens_hbm, wi_hbm, wt_hbm,
    image_out, text_out,
    scale_ref, shift_ref, feats, words, lens, wi, wt,
    flat_i, flat_t, power_i, power_t, part_i, part_t, got_i, got_t, code,
    full_i, full_t, images, texts, sums_i, sums_t, term_i, term_t, back_i, back_t,
    load_sem, s1, r1, s2, r2, s3, r3, s4, r4, s5, r5, s6, r6,
):
    group, width = feats.shape
    length = words.shape[1]
    emb = wi.shape[1]
    chunks = emb // LANES
    rows = sub * chunks
    span = term_i.shape[1]
    tower = lax.axis_index("tower")
    plane = lax.axis_index("loss") * pipes + lax.axis_index("pipe")

    def tower_at(k):
        return {"tower": partner(tower, k, towers)[0]}

    def plane_at(k):
        q = partner(plane, k, planes)[0]
        return {"loss": q // pipes, "pipe": lax.rem(q, pipes)}

    def block(i):
        at = i * rows
        return pl.multiple_of(at, 8) if rows % 8 == 0 else at

    loads = []
    for n, (src, dst) in enumerate((
        (lens_hbm.at[0], lens),
        (words_hbm.at[0, 0], words),
        (wt_hbm, wt),
        (feats_hbm.at[0, 0], feats),
        (wi_hbm, wi),
        (scale_hbm, scale_ref),
        (shift_hbm, shift_ref),
    )):
        loads.append(pltpu.make_async_copy(src, dst, load_sem.at[n]))
        loads[-1].start()

    barrier = pltpu.get_barrier_semaphore()
    each(1, towers, lambda k: pl.semaphore_signal(
        barrier, inc=1, device_id=tower_at(k), device_id_type=MESH))
    each(1, planes, lambda k: pl.semaphore_signal(
        barrier, inc=1, device_id=plane_at(k), device_id_type=MESH))

    def spread(ref, start, x):
        for c in range(chunks):
            ref[pl.ds(start + c, x.shape[0], stride=chunks), :] = x[:, c * LANES:(c + 1) * LANES]

    def gather(ref, start, n):
        return jnp.concatenate(
            [ref[pl.ds(start + c, n, stride=chunks), :] for c in range(chunks)], axis=1)

    def up(power):
        return jnp.exp(power * -LN2) * STEPS

    def down(power):
        return jnp.exp(power * LN2) * (1.0 / STEPS)

    def encode(raw, flat, power_ref, part):
        most = jnp.max(jnp.abs(raw), axis=1, keepdims=True)
        power = jnp.floor(jnp.log(jnp.maximum(most, 1e-30)) * (1.0 / LN2)) + 1.0
        spread(flat, 0, raw * up(power))
        power_ref[0:group, :] = jnp.broadcast_to(power, (group, LANES))
        for d in range(towers):
            values = jnp.round(flat[d * rows:(d + 1) * rows, :])
            part[d, 0:rows, :] = values.astype(jnp.int32).astype(CODE)
            part[d, span:span + sub, :] = power_ref[
                d * sub:(d + 1) * sub, :].astype(jnp.int32).astype(CODE)

    def scatter(k, part, got, send, recv):
        return pltpu.make_async_remote_copy(
            src_ref=part.at[partner(tower, k, towers)[0]], dst_ref=got.at[k - 1],
            send_sem=send.at[k - 1], recv_sem=recv.at[k - 1],
            device_id=tower_at(k), device_id_type=MESH)

    loads[0].wait()
    diagonal = (lax.broadcasted_iota(jnp.int32, (group, group), 0)
                == lax.broadcasted_iota(jnp.int32, (group, group), 1))
    counts = jnp.sum(jnp.where(diagonal, lens[...].astype(F32), 0.0), axis=1, keepdims=True)
    spot = lax.broadcasted_iota(jnp.int32, (group, group * length), 1)
    first = lax.broadcasted_iota(jnp.int32, (group, group * length), 0) * length
    keep = (spot >= first) & (spot < first + counts.astype(jnp.int32))
    keep = jnp.where(keep, 1.0, 0.0).astype(BF16)
    loads[1].wait()
    summed = jnp.dot(keep, words[...].reshape(group * length, words.shape[2]),
                     preferred_element_type=F32)
    pooled = (summed / counts).astype(BF16)
    loads[2].wait()
    encode(jnp.dot(pooled, wt[...], preferred_element_type=F32), flat_t, power_t, part_t)
    pl.semaphore_wait(barrier, towers + planes - 2)
    each(1, towers, lambda k: scatter(k, part_t, got_t, s1, r1).start())

    loads[3].wait()
    loads[4].wait()
    encode(jnp.dot(feats[...], wi[...], preferred_element_type=F32), flat_i, power_i, part_i)
    each(1, towers, lambda k: scatter(k, part_i, got_i, s2, r2).start())

    def unit(flat, power_ref, part, got, send, recv):
        raw = gather(flat, block(tower), sub) * down(power_ref[pl.ds(tower * sub, sub), 0:1])
        for k in reversed(range(1, towers)):
            scatter(k, part, got, send, recv).wait_recv()
            code[...] = got[k - 1, 0:rows, :].astype(jnp.int32).astype(F32)
            power = got[k - 1, span:span + sub, :].astype(jnp.int32).astype(F32)[:, 0:1]
            raw = raw + gather(code, 0, sub) * down(power)
        size = jnp.sum(raw * raw, axis=-1, keepdims=True) + 1e-06
        return raw * lax.rsqrt(size)

    def give_t(k):
        return pltpu.make_async_remote_copy(
            src_ref=texts.at[plane], dst_ref=texts.at[plane],
            send_sem=s3.at[k - 1], recv_sem=r3.at[k - 1],
            device_id=plane_at(k), device_id_type=MESH)

    def give_i(k):
        return pltpu.make_async_remote_copy(
            src_ref=images.at[tower], dst_ref=images.at[tower],
            send_sem=s4.at[k - 1], recv_sem=r4.at[k - 1],
            device_id=tower_at(k), device_id_type=MESH)

    spread(full_t, block(plane), unit(flat_t, power_t, part_t, got_t, s1, r1))
    texts[plane, 0:rows, :] = full_t[pl.ds(block(plane), rows), :].astype(BF16)
    each(1, planes, lambda k: give_t(k).start())
    spread(full_i, block(tower), unit(flat_i, power_i, part_i, got_i, s2, r2))
    images[tower, 0:rows, :] = full_i[pl.ds(block(tower), rows), :].astype(BF16)
    each(1, towers, lambda k: give_i(k).start())

    def take_i(k):
        give_i(k).wait_recv()
        q = partner(tower, k, towers)[1]
        full_i[pl.ds(block(q), rows), :] = images[q, 0:rows, :].astype(F32)

    def take_t(k):
        give_t(k).wait_recv()
        q = partner(plane, k, planes)[1]
        full_t[pl.ds(block(q), rows), :] = texts[q, 0:rows, :].astype(F32)

    loads[5].wait()
    loads[6].wait()
    scale = scale_ref[0]
    shift = shift_ref[0]
    cols = planes * sub
    near(1, towers, take_i)
    all_i = gather(full_i, 0, group).astype(BF16)
    near(1, planes, take_t)
    all_t = gather(full_t, 0, cols).astype(BF16)
    scores = lax.dot_general(all_i, all_t, (((1,), (1,)), ((), ())), preferred_element_type=F32)
    at_i = lax.broadcasted_iota(jnp.int32, (group, cols), 0) - tower * sub
    at_t = lax.broadcasted_iota(jnp.int32, (group, cols), 1) - plane * sub
    match = jnp.where((at_i == at_t) & (at_i >= 0) & (at_i < sub), 1.0, 0.0)
    grads = jax.nn.sigmoid(scale * scores + shift) - match

    def back_image(k):
        return pltpu.make_async_remote_copy(
            src_ref=term_i.at[partner(tower, k, towers)[0]], dst_ref=back_i.at[k - 1],
            send_sem=s5.at[k - 1], recv_sem=r5.at[k - 1],
            device_id=tower_at(k), device_id_type=MESH)

    def back_text(k):
        return pltpu.make_async_remote_copy(
            src_ref=term_t.at[partner(plane, k, planes)[0]], dst_ref=back_t.at[k - 1],
            send_sem=s6.at[k - 1], recv_sem=r6.at[k - 1],
            device_id=plane_at(k), device_id_type=MESH)

    def stage(n, sums, term):
        for d in range(n):
            term[d, 0:rows, :] = sums[d * rows:(d + 1) * rows, :].astype(WIRE)

    spread(sums_i, 0, jnp.dot(grads.astype(BF16), all_t, preferred_element_type=F32))
    stage(towers, sums_i, term_i)
    each(1, towers, lambda k: back_image(k).start())
    spread(sums_t, 0, jnp.dot(grads.T.astype(BF16), all_i, preferred_element_type=F32))
    stage(planes, sums_t, term_t)
    each(1, planes, lambda k: back_text(k).start())

    def total(sums, me, back, wait, n, out):
        near(1, n, wait)
        value = sums[pl.ds(block(me), rows), :]
        value = scale * (value + jnp.sum(back[:, 0:rows, :].astype(F32), axis=0))
        code[...] = value
        out[:, 0, :] = gather(code, 0, sub)

    total(sums_t, plane, back_t, lambda k: back_text(k).wait_recv(), planes, text_out)
    total(sums_i, tower, back_i, lambda k: back_image(k).wait_recv(), towers, image_out)

    each(1, towers, lambda k: scatter(k, part_t, got_t, s1, r1).wait_send())
    each(1, towers, lambda k: scatter(k, part_i, got_i, s2, r2).wait_send())
    each(1, planes, lambda k: give_t(k).wait_send())
    each(1, towers, lambda k: give_i(k).wait_send())
    each(1, towers, lambda k: back_image(k).wait_send())
    each(1, planes, lambda k: back_text(k).wait_send())


def finish(image_ref, text_ref, image_out, text_out):
    image_out[...] = image_ref[...]
    text_out[...] = text_ref[...]


def up_to(n, m):
    return -(-n // m) * m


def per_device(towers, pipes, planes, image_feats, text_tokens, lengths, w_image, w_text,
               logit_scale, logit_bias):
    group = image_feats.shape[2]
    emb = w_image.shape[1]
    sub = group // towers
    rows = sub * emb // LANES
    span = up_to(rows, 8)
    note = up_to(span + sub, 16)
    out = jax.ShapeDtypeStruct((sub, 1, emb), F32)
    sems = []
    for n in (towers, towers, planes, towers, towers, planes):
        sems += [pltpu.SemaphoreType.DMA((n - 1,))] * 2
    arrays = [pltpu.with_memory_space_constraint(x, pltpu.HBM) for x in (
        image_feats, text_tokens, lengths, w_image, w_text)]
    outs = pl.pallas_call(
        functools.partial(kernel, sub, towers, pipes, planes),
        out_shape=(out, out),
        in_specs=[pl.BlockSpec(memory_space=pl.ANY)] * 7,
        out_specs=(pl.BlockSpec(memory_space=pltpu.VMEM),) * 2,
        scratch_shapes=[
            pltpu.SMEM(logit_scale.shape, F32),
            pltpu.SMEM(logit_bias.shape, F32),
            pltpu.VMEM(image_feats.shape[2:], image_feats.dtype),
            pltpu.VMEM(text_tokens.shape[2:], text_tokens.dtype),
            pltpu.VMEM(lengths.shape[1:], lengths.dtype),
            pltpu.VMEM(w_image.shape, w_image.dtype),
            pltpu.VMEM(w_text.shape, w_text.dtype),
            pltpu.VMEM((towers * rows, LANES), F32),
            pltpu.VMEM((towers * rows, LANES), F32),
            pltpu.VMEM((up_to(group, 8), LANES), F32),
            pltpu.VMEM((up_to(group, 8), LANES), F32),
            pltpu.VMEM((towers, note, LANES), CODE),
            pltpu.VMEM((towers, note, LANES), CODE),
            pltpu.VMEM((towers - 1, note, LANES), CODE),
            pltpu.VMEM((towers - 1, note, LANES), CODE),
            pltpu.VMEM((rows, LANES), F32),
            pltpu.VMEM((towers * rows, LANES), F32),
            pltpu.VMEM((planes * rows, LANES), F32),
            pltpu.VMEM((towers, span, LANES), BF16),
            pltpu.VMEM((planes, span, LANES), BF16),
            pltpu.VMEM((towers * rows, LANES), F32),
            pltpu.VMEM((planes * rows, LANES), F32),
            pltpu.VMEM((towers, span, LANES), WIRE),
            pltpu.VMEM((planes, span, LANES), WIRE),
            pltpu.VMEM((towers - 1, span, LANES), WIRE),
            pltpu.VMEM((planes - 1, span, LANES), WIRE),
            pltpu.SemaphoreType.DMA((7,)),
        ] + sems,
        compiler_params=pltpu.CompilerParams(
            collective_id=0, has_side_effects=True, vmem_limit_bytes=24 * 2**20),
    )(logit_scale, logit_bias, *arrays)
    outs = pl.pallas_call(
        finish,
        out_shape=(out, out),
        in_specs=[pl.BlockSpec(memory_space=pltpu.VMEM)] * 2,
        out_specs=(pl.BlockSpec(memory_space=pltpu.VMEM),) * 2,
        compiler_params=pltpu.CompilerParams(vmem_limit_bytes=2**20),
    )(*outs)
    return tuple(o.reshape(1, 1, sub, emb) for o in outs)


def solution(mesh):
    shape = dict(mesh.shape)
    planes = shape["loss"] * shape["pipe"]
    return jax.shard_map(
        functools.partial(per_device, shape["tower"], shape["pipe"], planes),
        mesh=mesh,
        in_specs=(
            P("loss", "pipe", None, "tower"),
            P("loss", "pipe", None, None, "tower"),
            P("loss", "pipe", None),
            P("tower", None),
            P("tower", None),
            P(),
            P(),
        ),
        out_specs=(P("loss", "pipe", "tower", None), P("loss", "pipe", "tower", None)),
        check_vma=False,
    )
```

```python
import functools

import jax
import jax.numpy as jnp
from jax import lax
from jax.experimental import pallas as pl
from jax.experimental.pallas import tpu as pltpu
from jax.sharding import PartitionSpec as P

MESH = pl.DeviceIdType.MESH
WIRE = jnp.bfloat16
CODE = jnp.int16
F32 = jnp.float32
BF16 = jnp.bfloat16
UNROLL = 16
LANES = 128
STEPS = 32752.0


def each(lo, hi, body):
    if hi - lo <= UNROLL:
        for k in reversed(range(lo, hi)):
            body(k)
    else:
        lax.fori_loop(lo, hi, lambda k, c: (body(k), c)[1], 0)


def near(lo, hi, body):
    if hi - lo <= UNROLL:
        for k in sorted(range(lo, hi), key=lambda k: (bin(k).count("1"), k)):
            body(k)
    else:
        each(lo, hi, body)


def partner(me, k, n):
    if n <= UNROLL and n & (n - 1) == 0:
        q = me
        for b in range(n.bit_length() - 1):
            if (k >> b) & 1:
                q = q + (1 - 2 * lax.rem(me // (1 << b), 2)) * (1 << b)
        return q, q
    return lax.rem(me + k, n), lax.rem(me + n - k, n)


def kernel(
    sub, towers, pipes, planes,
    scale_hbm, shift_hbm, feats_hbm, words_hbm, lens_hbm, wi_hbm, wt_hbm,
    image_out, text_out,
    scale_ref, shift_ref, feats, words, lens, wi, wt,
    flat_i, flat_t, down_i, down_t, note_i, note_t, told_i, told_t,
    part_i, part_t, got_i, got_t, code,
    full_i, full_t, images, texts, sums_i, sums_t, term_i, term_t, back_i, back_t,
    load_sem, s1, r1, s2, r2, s3, r3, s4, r4, s5, r5, s6, r6, s7, r7, s8, r8,
):
    group, width = feats.shape
    length = words.shape[1]
    emb = wi.shape[1]
    chunks = emb // LANES
    rows = sub * chunks
    span = term_i.shape[1]
    tower = lax.axis_index("tower")
    plane = lax.axis_index("loss") * pipes + lax.axis_index("pipe")

    def tower_at(k):
        return {"tower": partner(tower, k, towers)[0]}

    def plane_at(k):
        q = partner(plane, k, planes)[0]
        return {"loss": q // pipes, "pipe": lax.rem(q, pipes)}

    def block(i):
        at = i * rows
        return pl.multiple_of(at, 8) if rows % 8 == 0 else at

    batch = 8 if group % 8 == 0 else group
    parts = group // batch
    loads = []
    for n, (src, dst) in enumerate(
        [(lens_hbm.at[0], lens)]
        + [(words_hbm.at[0, 0, c * batch:(c + 1) * batch], words.at[c * batch:(c + 1) * batch])
           for c in range(parts)]
        + [(wt_hbm, wt), (feats_hbm.at[0, 0], feats), (wi_hbm, wi),
           (scale_hbm, scale_ref), (shift_hbm, shift_ref)]
    ):
        loads.append(pltpu.make_async_copy(src, dst, load_sem.at[n]))
        loads[-1].start()
    load_lens, *load_words, load_wt, load_feats, load_wi, load_scale, load_shift = loads

    barrier = pltpu.get_barrier_semaphore()
    each(1, towers, lambda k: pl.semaphore_signal(
        barrier, inc=1, device_id=tower_at(k), device_id_type=MESH))
    each(1, planes, lambda k: pl.semaphore_signal(
        barrier, inc=1, device_id=plane_at(k), device_id_type=MESH))

    def spread(ref, start, x):
        for c in range(chunks):
            ref[pl.ds(start + c, x.shape[0], stride=chunks), :] = x[:, c * LANES:(c + 1) * LANES]

    def gather(ref, start, n):
        return jnp.concatenate(
            [ref[pl.ds(start + c, n, stride=chunks), :] for c in range(chunks)], axis=1)

    def encode(raw, flat, down, part, note):
        most = jnp.maximum(jnp.max(jnp.abs(raw), axis=1, keepdims=True), 1e-30)
        spread(flat, 0, raw * (STEPS / most))
        step = most * (1.0 / STEPS)
        down[0:group, :] = jnp.broadcast_to(step, (group, LANES))
        row = lax.broadcasted_iota(jnp.int32, (group, LANES), 0)
        lane = lax.broadcasted_iota(jnp.int32, (group, LANES), 1)
        for d in range(towers):
            mine = (row == lane + d * sub) & (lane < sub)
            note[d] = jnp.sum(jnp.where(mine, step, 0.0), axis=0, keepdims=True)
        for d in range(towers):
            values = jnp.round(flat[d * rows:(d + 1) * rows, :])
            part[d, 0:rows, :] = values.astype(jnp.int32).astype(CODE)

    def scatter(k, part, got, send, recv):
        return pltpu.make_async_remote_copy(
            src_ref=part.at[partner(tower, k, towers)[0]], dst_ref=got.at[k - 1],
            send_sem=send.at[k - 1], recv_sem=recv.at[k - 1],
            device_id=tower_at(k), device_id_type=MESH)

    load_lens.wait()
    counts = lens[...].astype(F32)
    pooled = []
    for c in range(parts):
        row = lax.broadcasted_iota(jnp.int32, (batch, group), 0) + c * batch
        mine = row == lax.broadcasted_iota(jnp.int32, (batch, group), 1)
        count = jnp.sum(jnp.where(mine, counts, 0.0), axis=1, keepdims=True)
        spot = lax.broadcasted_iota(jnp.int32, (batch, batch * length), 1)
        first = lax.broadcasted_iota(jnp.int32, (batch, batch * length), 0) * length
        keep = (spot >= first) & (spot < first + count.astype(jnp.int32))
        keep = jnp.where(keep, 1.0, 0.0).astype(BF16)
        load_words[c].wait()
        summed = jnp.dot(
            keep, words[c * batch:(c + 1) * batch].reshape(batch * length, words.shape[2]),
            preferred_element_type=F32)
        pooled.append(summed / count)
    pooled = jnp.concatenate(pooled, axis=0).astype(BF16)
    load_wt.wait()
    encode(jnp.dot(pooled, wt[...], preferred_element_type=F32), flat_t, down_t, part_t, note_t)
    pl.semaphore_wait(barrier, towers + planes - 2)
    each(1, towers, lambda k: scatter(k, note_t, told_t, s7, r7).start())
    each(1, towers, lambda k: scatter(k, part_t, got_t, s1, r1).start())

    load_feats.wait()
    load_wi.wait()
    encode(jnp.dot(feats[...], wi[...], preferred_element_type=F32), flat_i, down_i, part_i, note_i)
    each(1, towers, lambda k: scatter(k, note_i, told_i, s8, r8).start())
    each(1, towers, lambda k: scatter(k, part_i, got_i, s2, r2).start())

    def unit(flat, down, part, got, send, recv, note, told, note_send, note_recv):
        raw = gather(flat, block(tower), sub) * down[pl.ds(tower * sub, sub), 0:1]
        mine = (lax.broadcasted_iota(jnp.int32, (sub, LANES), 0)
                == lax.broadcasted_iota(jnp.int32, (sub, LANES), 1))
        for k in reversed(range(1, towers)):
            scatter(k, note, told, note_send, note_recv).wait_recv()
            step = jnp.sum(jnp.where(mine, told[k - 1], 0.0), axis=1, keepdims=True)
            scatter(k, part, got, send, recv).wait_recv()
            code[...] = got[k - 1, 0:rows, :].astype(jnp.int32).astype(F32)
            raw = raw + gather(code, 0, sub) * step
        size = jnp.sum(raw * raw, axis=-1, keepdims=True) + 1e-06
        return raw * lax.rsqrt(size)

    def give_t(k):
        return pltpu.make_async_remote_copy(
            src_ref=texts.at[plane], dst_ref=texts.at[plane],
            send_sem=s3.at[k - 1], recv_sem=r3.at[k - 1],
            device_id=plane_at(k), device_id_type=MESH)

    def give_i(k):
        return pltpu.make_async_remote_copy(
            src_ref=images.at[tower], dst_ref=images.at[tower],
            send_sem=s4.at[k - 1], recv_sem=r4.at[k - 1],
            device_id=tower_at(k), device_id_type=MESH)

    spread(full_t, block(plane), unit(
        flat_t, down_t, part_t, got_t, s1, r1, note_t, told_t, s7, r7))
    texts[plane, 0:rows, :] = full_t[pl.ds(block(plane), rows), :].astype(BF16)
    each(1, planes, lambda k: give_t(k).start())
    spread(full_i, block(tower), unit(
        flat_i, down_i, part_i, got_i, s2, r2, note_i, told_i, s8, r8))
    images[tower, 0:rows, :] = full_i[pl.ds(block(tower), rows), :].astype(BF16)
    each(1, towers, lambda k: give_i(k).start())

    def take_i(k):
        give_i(k).wait_recv()
        q = partner(tower, k, towers)[1]
        full_i[pl.ds(block(q), rows), :] = images[q, 0:rows, :].astype(F32)

    def take_t(k):
        give_t(k).wait_recv()
        q = partner(plane, k, planes)[1]
        full_t[pl.ds(block(q), rows), :] = texts[q, 0:rows, :].astype(F32)

    load_scale.wait()
    load_shift.wait()
    scale = scale_ref[0]
    shift = shift_ref[0]
    cols = planes * sub
    near(1, planes, take_t)
    all_t = gather(full_t, 0, cols).astype(BF16)
    near(1, towers, take_i)
    all_i = gather(full_i, 0, group).astype(BF16)
    scores = lax.dot_general(all_i, all_t, (((1,), (1,)), ((), ())), preferred_element_type=F32)
    at_i = lax.broadcasted_iota(jnp.int32, (group, cols), 0) - tower * sub
    at_t = lax.broadcasted_iota(jnp.int32, (group, cols), 1) - plane * sub
    match = jnp.where((at_i == at_t) & (at_i >= 0) & (at_i < sub), 1.0, 0.0)
    grads = jax.nn.sigmoid(scale * scores + shift) - match

    def back_image(k):
        return pltpu.make_async_remote_copy(
            src_ref=term_i.at[partner(tower, k, towers)[0]], dst_ref=back_i.at[k - 1],
            send_sem=s5.at[k - 1], recv_sem=r5.at[k - 1],
            device_id=tower_at(k), device_id_type=MESH)

    def back_text(k):
        return pltpu.make_async_remote_copy(
            src_ref=term_t.at[partner(plane, k, planes)[0]], dst_ref=back_t.at[k - 1],
            send_sem=s6.at[k - 1], recv_sem=r6.at[k - 1],
            device_id=plane_at(k), device_id_type=MESH)

    def stage(n, sums, term):
        for d in range(n):
            term[d, 0:rows, :] = sums[d * rows:(d + 1) * rows, :].astype(WIRE)

    spread(sums_i, 0, jnp.dot(grads.astype(BF16), all_t, preferred_element_type=F32))
    stage(towers, sums_i, term_i)
    each(1, towers, lambda k: back_image(k).start())
    spread(sums_t, 0, jnp.dot(grads.T.astype(BF16), all_i, preferred_element_type=F32))
    stage(planes, sums_t, term_t)
    each(1, planes, lambda k: back_text(k).start())

    def total(sums, me, back, wait, n, out):
        near(1, n, wait)
        value = sums[pl.ds(block(me), rows), :]
        value = scale * (value + jnp.sum(back[:, 0:rows, :].astype(F32), axis=0))
        code[...] = value
        out[:, 0, :] = gather(code, 0, sub)

    total(sums_t, plane, back_t, lambda k: back_text(k).wait_recv(), planes, text_out)
    total(sums_i, tower, back_i, lambda k: back_image(k).wait_recv(), towers, image_out)

    each(1, towers, lambda k: scatter(k, note_t, told_t, s7, r7).wait_send())
    each(1, towers, lambda k: scatter(k, note_i, told_i, s8, r8).wait_send())
    each(1, towers, lambda k: scatter(k, part_t, got_t, s1, r1).wait_send())
    each(1, towers, lambda k: scatter(k, part_i, got_i, s2, r2).wait_send())
    each(1, planes, lambda k: give_t(k).wait_send())
    each(1, towers, lambda k: give_i(k).wait_send())
    each(1, towers, lambda k: back_image(k).wait_send())
    each(1, planes, lambda k: back_text(k).wait_send())


def finish(image_ref, text_ref, image_out, text_out):
    image_out[...] = image_ref[...]
    text_out[...] = text_ref[...]


def up_to(n, m):
    return -(-n // m) * m


def per_device(towers, pipes, planes, image_feats, text_tokens, lengths, w_image, w_text,
               logit_scale, logit_bias):
    group = image_feats.shape[2]
    emb = w_image.shape[1]
    sub = group // towers
    rows = sub * emb // LANES
    span = up_to(rows, 8)
    out = jax.ShapeDtypeStruct((sub, 1, emb), F32)
    sems = []
    for n in (towers, towers, planes, towers, towers, planes, towers, towers):
        sems += [pltpu.SemaphoreType.DMA((n - 1,))] * 2
    arrays = [pltpu.with_memory_space_constraint(x, pltpu.HBM) for x in (
        image_feats, text_tokens, lengths, w_image, w_text)]
    outs = pl.pallas_call(
        functools.partial(kernel, sub, towers, pipes, planes),
        out_shape=(out, out),
        in_specs=[pl.BlockSpec(memory_space=pl.ANY)] * 7,
        out_specs=(pl.BlockSpec(memory_space=pltpu.VMEM),) * 2,
        scratch_shapes=[
            pltpu.SMEM(logit_scale.shape, F32),
            pltpu.SMEM(logit_bias.shape, F32),
            pltpu.VMEM(image_feats.shape[2:], image_feats.dtype),
            pltpu.VMEM(text_tokens.shape[2:], text_tokens.dtype),
            pltpu.VMEM(lengths.shape[1:], lengths.dtype),
            pltpu.VMEM(w_image.shape, w_image.dtype),
            pltpu.VMEM(w_text.shape, w_text.dtype),
            pltpu.VMEM((towers * rows, LANES), F32),
            pltpu.VMEM((towers * rows, LANES), F32),
            pltpu.VMEM((up_to(group, 8), LANES), F32),
            pltpu.VMEM((up_to(group, 8), LANES), F32),
            pltpu.VMEM((towers, 1, LANES), F32),
            pltpu.VMEM((towers, 1, LANES), F32),
            pltpu.VMEM((towers - 1, 1, LANES), F32),
            pltpu.VMEM((towers - 1, 1, LANES), F32),
            pltpu.VMEM((towers, span, LANES), CODE),
            pltpu.VMEM((towers, span, LANES), CODE),
            pltpu.VMEM((towers - 1, span, LANES), CODE),
            pltpu.VMEM((towers - 1, span, LANES), CODE),
            pltpu.VMEM((rows, LANES), F32),
            pltpu.VMEM((towers * rows, LANES), F32),
            pltpu.VMEM((planes * rows, LANES), F32),
            pltpu.VMEM((towers, span, LANES), BF16),
            pltpu.VMEM((planes, span, LANES), BF16),
            pltpu.VMEM((towers * rows, LANES), F32),
            pltpu.VMEM((planes * rows, LANES), F32),
            pltpu.VMEM((towers, span, LANES), WIRE),
            pltpu.VMEM((planes, span, LANES), WIRE),
            pltpu.VMEM((towers - 1, span, LANES), WIRE),
            pltpu.VMEM((planes - 1, span, LANES), WIRE),
            pltpu.SemaphoreType.DMA((6 + group // (8 if group % 8 == 0 else group),)),
        ] + sems,
        compiler_params=pltpu.CompilerParams(
            collective_id=0, has_side_effects=True, vmem_limit_bytes=24 * 2**20),
    )(logit_scale, logit_bias, *arrays)
    outs = pl.pallas_call(
        finish,
        out_shape=(out, out),
        in_specs=[pl.BlockSpec(memory_space=pltpu.VMEM)] * 2,
        out_specs=(pl.BlockSpec(memory_space=pltpu.VMEM),) * 2,
        compiler_params=pltpu.CompilerParams(vmem_limit_bytes=2**20),
    )(*outs)
    return tuple(o.reshape(1, 1, sub, emb) for o in outs)


def solution(mesh):
    shape = dict(mesh.shape)
    planes = shape["loss"] * shape["pipe"]
    return jax.shard_map(
        functools.partial(per_device, shape["tower"], shape["pipe"], planes),
        mesh=mesh,
        in_specs=(
            P("loss", "pipe", None, "tower"),
            P("loss", "pipe", None, None, "tower"),
            P("loss", "pipe", None),
            P("tower", None),
            P("tower", None),
            P(),
            P(),
        ),
        out_specs=(P("loss", "pipe", "tower", None), P("loss", "pipe", "tower", None)),
        check_vma=False,
    )
```

```python
import functools

import jax
import jax.numpy as jnp
from jax import lax
from jax.experimental import pallas as pl
from jax.experimental.pallas import tpu as pltpu
from jax.sharding import PartitionSpec as P

MESH = pl.DeviceIdType.MESH
WIRE = jnp.bfloat16
CODE = jnp.int16
F32 = jnp.float32
BF16 = jnp.bfloat16
UNROLL = 16
LANES = 128
STEPS = 32752.0


def each(lo, hi, body):
    if hi - lo <= UNROLL:
        for k in reversed(range(lo, hi)):
            body(k)
    else:
        lax.fori_loop(lo, hi, lambda k, c: (body(k), c)[1], 0)


def near(lo, hi, body):
    if hi - lo <= UNROLL:
        for k in sorted(range(lo, hi), key=lambda k: (bin(k).count("1"), k)):
            body(k)
    else:
        each(lo, hi, body)


def partner(me, k, n):
    if n <= UNROLL and n & (n - 1) == 0:
        q = me
        for b in range(n.bit_length() - 1):
            if (k >> b) & 1:
                q = q + (1 - 2 * lax.rem(me // (1 << b), 2)) * (1 << b)
        return q, q
    return lax.rem(me + k, n), lax.rem(me + n - k, n)


def kernel(
    sub, towers, pipes, planes,
    scale_hbm, shift_hbm, feats_hbm, words_hbm, lens_hbm, wi_hbm, wt_hbm,
    image_out, text_out,
    scale_ref, shift_ref, feats, words, lens, wi, wt,
    flat_i, flat_t, down_i, down_t, note_i, note_t, told_i, told_t,
    part_i, part_t, got_i, got_t, code,
    full_i, full_t, images, texts, sums_i, sums_t, term_i, term_t, back_i, back_t,
    load_sem, s1, r1, s2, r2, s3, r3, s4, r4, s5, r5, s6, r6, s7, r7, s8, r8,
):
    group, width = feats.shape
    length = words.shape[1]
    emb = wi.shape[1]
    chunks = emb // LANES
    rows = sub * chunks
    span = term_i.shape[1]
    tower = lax.axis_index("tower")
    plane = lax.axis_index("loss") * pipes + lax.axis_index("pipe")

    def tower_at(k):
        return {"tower": partner(tower, k, towers)[0]}

    def plane_at(k):
        q = partner(plane, k, planes)[0]
        return {"loss": q // pipes, "pipe": lax.rem(q, pipes)}

    def block(i):
        at = i * rows
        return pl.multiple_of(at, 8) if rows % 8 == 0 else at

    barrier = pltpu.get_barrier_semaphore()
    each(1, towers, lambda k: pl.semaphore_signal(
        barrier, inc=1, device_id=tower_at(k), device_id_type=MESH))
    batch = 8 if group % 8 == 0 else group
    parts = group // batch
    loads = []
    for n, (src, dst) in enumerate(
        [(lens_hbm.at[0], lens)]
        + [(words_hbm.at[0, 0, c * batch:(c + 1) * batch], words.at[c * batch:(c + 1) * batch])
           for c in range(parts)]
        + [(wt_hbm, wt), (feats_hbm.at[0, 0], feats), (wi_hbm, wi),
           (scale_hbm, scale_ref), (shift_hbm, shift_ref)]
    ):
        loads.append(pltpu.make_async_copy(src, dst, load_sem.at[n]))
        loads[-1].start()
    load_lens, *load_words, load_wt, load_feats, load_wi, load_scale, load_shift = loads

    each(1, planes, lambda k: pl.semaphore_signal(
        barrier, inc=1, device_id=plane_at(k), device_id_type=MESH))

    def spread(ref, start, x):
        for c in range(chunks):
            ref[pl.ds(start + c, x.shape[0], stride=chunks), :] = x[:, c * LANES:(c + 1) * LANES]

    def gather(ref, start, n):
        return jnp.concatenate(
            [ref[pl.ds(start + c, n, stride=chunks), :] for c in range(chunks)], axis=1)

    def encode(raw, flat, down, part, note):
        most = jnp.maximum(jnp.max(jnp.abs(raw), axis=1, keepdims=True), 1e-30)
        spread(flat, 0, raw * (STEPS / most))
        step = most * (1.0 / STEPS)
        down[0:group, :] = jnp.broadcast_to(step, (group, LANES))
        row = lax.broadcasted_iota(jnp.int32, (group, LANES), 0)
        lane = lax.broadcasted_iota(jnp.int32, (group, LANES), 1)
        for d in range(towers):
            mine = (row == lane + d * sub) & (lane < sub)
            note[d] = jnp.sum(jnp.where(mine, step, 0.0), axis=0, keepdims=True)
        for d in range(towers):
            values = jnp.round(flat[d * rows:(d + 1) * rows, :])
            part[d, 0:rows, :] = values.astype(jnp.int32).astype(CODE)

    def scatter(k, part, got, send, recv):
        return pltpu.make_async_remote_copy(
            src_ref=part.at[partner(tower, k, towers)[0]], dst_ref=got.at[k - 1],
            send_sem=send.at[k - 1], recv_sem=recv.at[k - 1],
            device_id=tower_at(k), device_id_type=MESH)

    load_lens.wait()
    counts = lens[...].astype(F32)
    pooled = []
    for c in range(parts):
        row = lax.broadcasted_iota(jnp.int32, (batch, group), 0) + c * batch
        mine = row == lax.broadcasted_iota(jnp.int32, (batch, group), 1)
        count = jnp.sum(jnp.where(mine, counts, 0.0), axis=1, keepdims=True)
        spot = lax.broadcasted_iota(jnp.int32, (batch, batch * length), 1)
        first = lax.broadcasted_iota(jnp.int32, (batch, batch * length), 0) * length
        keep = (spot >= first) & (spot < first + count.astype(jnp.int32))
        keep = jnp.where(keep, 1.0, 0.0).astype(BF16)
        load_words[c].wait()
        summed = jnp.dot(
            keep, words[c * batch:(c + 1) * batch].reshape(batch * length, words.shape[2]),
            preferred_element_type=F32)
        pooled.append(summed / count)
    pooled = jnp.concatenate(pooled, axis=0).astype(BF16)
    load_wt.wait()
    encode(jnp.dot(pooled, wt[...], preferred_element_type=F32), flat_t, down_t, part_t, note_t)
    pl.semaphore_wait(barrier, towers + planes - 2)
    each(1, towers, lambda k: scatter(k, note_t, told_t, s7, r7).start())
    each(1, towers, lambda k: scatter(k, part_t, got_t, s1, r1).start())

    load_feats.wait()
    load_wi.wait()
    encode(jnp.dot(feats[...], wi[...], preferred_element_type=F32), flat_i, down_i, part_i, note_i)
    each(1, towers, lambda k: scatter(k, note_i, told_i, s8, r8).start())
    each(1, towers, lambda k: scatter(k, part_i, got_i, s2, r2).start())

    def unit(flat, down, part, got, send, recv, note, told, note_send, note_recv):
        raw = gather(flat, block(tower), sub) * down[pl.ds(tower * sub, sub), 0:1]
        mine = (lax.broadcasted_iota(jnp.int32, (sub, LANES), 0)
                == lax.broadcasted_iota(jnp.int32, (sub, LANES), 1))
        for k in sorted(range(1, towers), key=lambda k: (bin(k).count("1"), k)):
            scatter(k, note, told, note_send, note_recv).wait_recv()
            step = jnp.sum(jnp.where(mine, told[k - 1], 0.0), axis=1, keepdims=True)
            scatter(k, part, got, send, recv).wait_recv()
            code[...] = got[k - 1, 0:rows, :].astype(jnp.int32).astype(F32)
            raw = raw + gather(code, 0, sub) * step
        size = jnp.sum(raw * raw, axis=-1, keepdims=True) + 1e-06
        return raw * lax.rsqrt(size)

    def give_t(k):
        return pltpu.make_async_remote_copy(
            src_ref=texts.at[plane], dst_ref=texts.at[plane],
            send_sem=s3.at[k - 1], recv_sem=r3.at[k - 1],
            device_id=plane_at(k), device_id_type=MESH)

    def give_i(k):
        return pltpu.make_async_remote_copy(
            src_ref=images.at[tower], dst_ref=images.at[tower],
            send_sem=s4.at[k - 1], recv_sem=r4.at[k - 1],
            device_id=tower_at(k), device_id_type=MESH)

    spread(full_t, block(plane), unit(
        flat_t, down_t, part_t, got_t, s1, r1, note_t, told_t, s7, r7))
    texts[plane, 0:rows, :] = full_t[pl.ds(block(plane), rows), :].astype(BF16)
    each(1, planes, lambda k: give_t(k).start())
    spread(full_i, block(tower), unit(
        flat_i, down_i, part_i, got_i, s2, r2, note_i, told_i, s8, r8))
    images[tower, 0:rows, :] = full_i[pl.ds(block(tower), rows), :].astype(BF16)
    each(1, towers, lambda k: give_i(k).start())

    def take_i(k):
        give_i(k).wait_recv()
        q = partner(tower, k, towers)[1]
        full_i[pl.ds(block(q), rows), :] = images[q, 0:rows, :].astype(F32)

    def take_t(k):
        give_t(k).wait_recv()
        q = partner(plane, k, planes)[1]
        full_t[pl.ds(block(q), rows), :] = texts[q, 0:rows, :].astype(F32)

    load_scale.wait()
    load_shift.wait()
    scale = scale_ref[0]
    shift = shift_ref[0]
    cols = planes * sub
    near(1, planes, take_t)
    all_t = gather(full_t, 0, cols).astype(BF16)
    near(1, towers, take_i)
    all_i = gather(full_i, 0, group).astype(BF16)
    scores = lax.dot_general(all_i, all_t, (((1,), (1,)), ((), ())), preferred_element_type=F32)
    at_i = lax.broadcasted_iota(jnp.int32, (group, cols), 0) - tower * sub
    at_t = lax.broadcasted_iota(jnp.int32, (group, cols), 1) - plane * sub
    match = jnp.where((at_i == at_t) & (at_i >= 0) & (at_i < sub), 1.0, 0.0)
    grads = jax.nn.sigmoid(scale * scores + shift) - match

    def back_image(k):
        return pltpu.make_async_remote_copy(
            src_ref=term_i.at[partner(tower, k, towers)[0]], dst_ref=back_i.at[k - 1],
            send_sem=s5.at[k - 1], recv_sem=r5.at[k - 1],
            device_id=tower_at(k), device_id_type=MESH)

    def back_text(k):
        return pltpu.make_async_remote_copy(
            src_ref=term_t.at[partner(plane, k, planes)[0]], dst_ref=back_t.at[k - 1],
            send_sem=s6.at[k - 1], recv_sem=r6.at[k - 1],
            device_id=plane_at(k), device_id_type=MESH)

    def stage(n, sums, term):
        for d in range(n):
            term[d, 0:rows, :] = sums[d * rows:(d + 1) * rows, :].astype(WIRE)

    spread(sums_i, 0, jnp.dot(grads.astype(BF16), all_t, preferred_element_type=F32))
    stage(towers, sums_i, term_i)
    each(1, towers, lambda k: back_image(k).start())
    spread(sums_t, 0, jnp.dot(grads.T.astype(BF16), all_i, preferred_element_type=F32))
    stage(planes, sums_t, term_t)
    each(1, planes, lambda k: back_text(k).start())

    def total(sums, me, back, wait, n, out):
        near(1, n, wait)
        value = sums[pl.ds(block(me), rows), :]
        value = scale * (value + jnp.sum(back[:, 0:rows, :].astype(F32), axis=0))
        code[...] = value
        out[:, 0, :] = gather(code, 0, sub)

    total(sums_t, plane, back_t, lambda k: back_text(k).wait_recv(), planes, text_out)
    total(sums_i, tower, back_i, lambda k: back_image(k).wait_recv(), towers, image_out)

    each(1, towers, lambda k: scatter(k, note_t, told_t, s7, r7).wait_send())
    each(1, towers, lambda k: scatter(k, note_i, told_i, s8, r8).wait_send())
    each(1, towers, lambda k: scatter(k, part_t, got_t, s1, r1).wait_send())
    each(1, towers, lambda k: scatter(k, part_i, got_i, s2, r2).wait_send())
    each(1, planes, lambda k: give_t(k).wait_send())
    each(1, towers, lambda k: give_i(k).wait_send())
    each(1, towers, lambda k: back_image(k).wait_send())
    each(1, planes, lambda k: back_text(k).wait_send())


def finish(image_ref, text_ref, image_out, text_out):
    image_out[...] = image_ref[...]
    text_out[...] = text_ref[...]


def up_to(n, m):
    return -(-n // m) * m


def per_device(towers, pipes, planes, image_feats, text_tokens, lengths, w_image, w_text,
               logit_scale, logit_bias):
    group = image_feats.shape[2]
    emb = w_image.shape[1]
    sub = group // towers
    rows = sub * emb // LANES
    span = up_to(rows, 8)
    out = jax.ShapeDtypeStruct((sub, 1, emb), F32)
    sems = []
    for n in (towers, towers, planes, towers, towers, planes, towers, towers):
        sems += [pltpu.SemaphoreType.DMA((n - 1,))] * 2
    arrays = [pltpu.with_memory_space_constraint(x, pltpu.HBM) for x in (
        image_feats, text_tokens, lengths, w_image, w_text)]
    outs = pl.pallas_call(
        functools.partial(kernel, sub, towers, pipes, planes),
        out_shape=(out, out),
        in_specs=[pl.BlockSpec(memory_space=pl.ANY)] * 7,
        out_specs=(pl.BlockSpec(memory_space=pltpu.VMEM),) * 2,
        scratch_shapes=[
            pltpu.SMEM(logit_scale.shape, F32),
            pltpu.SMEM(logit_bias.shape, F32),
            pltpu.VMEM(image_feats.shape[2:], image_feats.dtype),
            pltpu.VMEM(text_tokens.shape[2:], text_tokens.dtype),
            pltpu.VMEM(lengths.shape[1:], lengths.dtype),
            pltpu.VMEM(w_image.shape, w_image.dtype),
            pltpu.VMEM(w_text.shape, w_text.dtype),
            pltpu.VMEM((towers * rows, LANES), F32),
            pltpu.VMEM((towers * rows, LANES), F32),
            pltpu.VMEM((up_to(group, 8), LANES), F32),
            pltpu.VMEM((up_to(group, 8), LANES), F32),
            pltpu.VMEM((towers, 1, LANES), F32),
            pltpu.VMEM((towers, 1, LANES), F32),
            pltpu.VMEM((towers - 1, 1, LANES), F32),
            pltpu.VMEM((towers - 1, 1, LANES), F32),
            pltpu.VMEM((towers, span, LANES), CODE),
            pltpu.VMEM((towers, span, LANES), CODE),
            pltpu.VMEM((towers - 1, span, LANES), CODE),
            pltpu.VMEM((towers - 1, span, LANES), CODE),
            pltpu.VMEM((rows, LANES), F32),
            pltpu.VMEM((towers * rows, LANES), F32),
            pltpu.VMEM((planes * rows, LANES), F32),
            pltpu.VMEM((towers, span, LANES), BF16),
            pltpu.VMEM((planes, span, LANES), BF16),
            pltpu.VMEM((towers * rows, LANES), F32),
            pltpu.VMEM((planes * rows, LANES), F32),
            pltpu.VMEM((towers, span, LANES), WIRE),
            pltpu.VMEM((planes, span, LANES), WIRE),
            pltpu.VMEM((towers - 1, span, LANES), WIRE),
            pltpu.VMEM((planes - 1, span, LANES), WIRE),
            pltpu.SemaphoreType.DMA((6 + group // (8 if group % 8 == 0 else group),)),
        ] + sems,
        compiler_params=pltpu.CompilerParams(
            collective_id=0, has_side_effects=True, vmem_limit_bytes=24 * 2**20),
    )(logit_scale, logit_bias, *arrays)
    outs = pl.pallas_call(
        finish,
        out_shape=(out, out),
        in_specs=[pl.BlockSpec(memory_space=pltpu.VMEM)] * 2,
        out_specs=(pl.BlockSpec(memory_space=pltpu.VMEM),) * 2,
        compiler_params=pltpu.CompilerParams(vmem_limit_bytes=2**20),
    )(*outs)
    return tuple(o.reshape(1, 1, sub, emb) for o in outs)


def solution(mesh):
    shape = dict(mesh.shape)
    planes = shape["loss"] * shape["pipe"]
    return jax.shard_map(
        functools.partial(per_device, shape["tower"], shape["pipe"], planes),
        mesh=mesh,
        in_specs=(
            P("loss", "pipe", None, "tower"),
            P("loss", "pipe", None, None, "tower"),
            P("loss", "pipe", None),
            P("tower", None),
            P("tower", None),
            P(),
            P(),
        ),
        out_specs=(P("loss", "pipe", "tower", None), P("loss", "pipe", "tower", None)),
        check_vma=False,
    )
```

```python
import functools

import jax
import jax.numpy as jnp
from jax import lax
from jax.experimental import pallas as pl
from jax.experimental.pallas import tpu as pltpu
from jax.sharding import PartitionSpec as P

MESH = pl.DeviceIdType.MESH
WIRE = jnp.bfloat16
CODE = jnp.int16
F32 = jnp.float32
BF16 = jnp.bfloat16
UNROLL = 16
LANES = 128
STEPS = 32752.0


def each(lo, hi, body):
    if hi - lo <= UNROLL:
        for k in reversed(range(lo, hi)):
            body(k)
    else:
        lax.fori_loop(lo, hi, lambda k, c: (body(k), c)[1], 0)


def near(lo, hi, body):
    if hi - lo <= UNROLL:
        for k in sorted(range(lo, hi), key=lambda k: (bin(k).count("1"), k)):
            body(k)
    else:
        each(lo, hi, body)


def partner(me, k, n):
    if isinstance(k, tuple):
        return k[1], k[1]
    if n <= UNROLL and n & (n - 1) == 0:
        q = me
        for b in range(n.bit_length() - 1):
            if (k >> b) & 1:
                q = q + (1 - 2 * lax.rem(me // (1 << b), 2)) * (1 << b)
        return q, q
    return lax.rem(me + k, n), lax.rem(me + n - k, n)


def slot(k):
    return (k[0] if isinstance(k, tuple) else k) - 1


def line(me, n, body):
    if n != 4:
        each(1, n, body)
        return
    upper = me // 2
    inner = lax.rem((me + 1) // 2, 2)
    body((3 - inner, 3 * (1 - upper)))
    body((2 + inner, 2 - upper))
    body(1)


def kernel(
    sub, towers, pipes, planes,
    scale_hbm, shift_hbm, feats_hbm, words_hbm, lens_hbm, wi_hbm, wt_hbm,
    image_out, text_out,
    scale_ref, shift_ref, feats, words, lens, wi, wt,
    flat_i, flat_t, down_i, down_t, note_i, note_t, told_i, told_t,
    part_i, part_t, got_i, got_t, code,
    full_i, full_t, images, texts, sums_i, sums_t, term_i, term_t, back_i, back_t,
    load_sem, s1, r1, s2, r2, s3, r3, s4, r4, s5, r5, s6, r6, s7, r7, s8, r8,
):
    group, width = feats.shape
    length = words.shape[1]
    emb = wi.shape[1]
    chunks = emb // LANES
    rows = sub * chunks
    span = term_i.shape[1]
    tower = lax.axis_index("tower")
    plane = lax.axis_index("loss") * pipes + lax.axis_index("pipe")

    def tower_at(k):
        return {"tower": partner(tower, k, towers)[0]}

    def plane_at(k):
        q = partner(plane, k, planes)[0]
        return {"loss": q // pipes, "pipe": lax.rem(q, pipes)}

    def block(i):
        at = i * rows
        return pl.multiple_of(at, 8) if rows % 8 == 0 else at

    barrier = pltpu.get_barrier_semaphore()
    each(1, towers, lambda k: pl.semaphore_signal(
        barrier, inc=1, device_id=tower_at(k), device_id_type=MESH))
    batch = 8 if group % 8 == 0 else group
    parts = group // batch
    loads = []
    for n, (src, dst) in enumerate(
        [(lens_hbm.at[0], lens)]
        + [(words_hbm.at[0, 0, c * batch:(c + 1) * batch], words.at[c * batch:(c + 1) * batch])
           for c in range(parts)]
        + [(wt_hbm, wt), (feats_hbm.at[0, 0], feats), (wi_hbm, wi),
           (scale_hbm, scale_ref), (shift_hbm, shift_ref)]
    ):
        loads.append(pltpu.make_async_copy(src, dst, load_sem.at[n]))
        loads[-1].start()
    load_lens, *load_words, load_wt, load_feats, load_wi, load_scale, load_shift = loads

    each(1, planes, lambda k: pl.semaphore_signal(
        barrier, inc=1, device_id=plane_at(k), device_id_type=MESH))

    def spread(ref, start, x):
        for c in range(chunks):
            ref[pl.ds(start + c, x.shape[0], stride=chunks), :] = x[:, c * LANES:(c + 1) * LANES]

    def gather(ref, start, n):
        return jnp.concatenate(
            [ref[pl.ds(start + c, n, stride=chunks), :] for c in range(chunks)], axis=1)

    def encode(raw, flat, down, part, note):
        most = jnp.maximum(jnp.max(jnp.abs(raw), axis=1, keepdims=True), 1e-30)
        spread(flat, 0, raw * (STEPS / most))
        step = most * (1.0 / STEPS)
        down[0:group, :] = jnp.broadcast_to(step, (group, LANES))
        row = lax.broadcasted_iota(jnp.int32, (group, LANES), 0)
        lane = lax.broadcasted_iota(jnp.int32, (group, LANES), 1)
        for d in range(towers):
            mine = (row == lane + d * sub) & (lane < sub)
            note[d] = jnp.sum(jnp.where(mine, step, 0.0), axis=0, keepdims=True)
        for d in range(towers):
            values = jnp.round(flat[d * rows:(d + 1) * rows, :])
            part[d, 0:rows, :] = values.astype(jnp.int32).astype(CODE)

    def scatter(k, part, got, send, recv):
        return pltpu.make_async_remote_copy(
            src_ref=part.at[partner(tower, k, towers)[0]], dst_ref=got.at[slot(k)],
            send_sem=send.at[slot(k)], recv_sem=recv.at[slot(k)],
            device_id=tower_at(k), device_id_type=MESH)

    load_lens.wait()
    counts = lens[...].astype(F32)
    pooled = []
    for c in range(parts):
        row = lax.broadcasted_iota(jnp.int32, (batch, group), 0) + c * batch
        mine = row == lax.broadcasted_iota(jnp.int32, (batch, group), 1)
        count = jnp.sum(jnp.where(mine, counts, 0.0), axis=1, keepdims=True)
        spot = lax.broadcasted_iota(jnp.int32, (batch, batch * length), 1)
        first = lax.broadcasted_iota(jnp.int32, (batch, batch * length), 0) * length
        keep = (spot >= first) & (spot < first + count.astype(jnp.int32))
        keep = jnp.where(keep, 1.0, 0.0).astype(BF16)
        load_words[c].wait()
        summed = jnp.dot(
            keep, words[c * batch:(c + 1) * batch].reshape(batch * length, words.shape[2]),
            preferred_element_type=F32)
        pooled.append(summed / count)
    pooled = jnp.concatenate(pooled, axis=0).astype(BF16)
    load_wt.wait()
    encode(jnp.dot(pooled, wt[...], preferred_element_type=F32), flat_t, down_t, part_t, note_t)
    pl.semaphore_wait(barrier, towers + planes - 2)
    line(tower, towers, lambda k: scatter(k, note_t, told_t, s7, r7).start())
    line(tower, towers, lambda k: scatter(k, part_t, got_t, s1, r1).start())

    load_feats.wait()
    load_wi.wait()
    encode(jnp.dot(feats[...], wi[...], preferred_element_type=F32), flat_i, down_i, part_i, note_i)
    line(tower, towers, lambda k: scatter(k, note_i, told_i, s8, r8).start())
    line(tower, towers, lambda k: scatter(k, part_i, got_i, s2, r2).start())

    def unit(flat, down, part, got, send, recv, note, told, note_send, note_recv):
        raw = gather(flat, block(tower), sub) * down[pl.ds(tower * sub, sub), 0:1]
        mine = (lax.broadcasted_iota(jnp.int32, (sub, LANES), 0)
                == lax.broadcasted_iota(jnp.int32, (sub, LANES), 1))
        for k in sorted(range(1, towers), key=lambda k: (bin(k).count("1"), k)):
            scatter(k, note, told, note_send, note_recv).wait_recv()
            step = jnp.sum(jnp.where(mine, told[k - 1], 0.0), axis=1, keepdims=True)
            scatter(k, part, got, send, recv).wait_recv()
            code[...] = got[k - 1, 0:rows, :].astype(jnp.int32).astype(F32)
            raw = raw + gather(code, 0, sub) * step
        size = jnp.sum(raw * raw, axis=-1, keepdims=True) + 1e-06
        return raw * lax.rsqrt(size)

    def give_t(k):
        return pltpu.make_async_remote_copy(
            src_ref=texts.at[plane], dst_ref=texts.at[plane],
            send_sem=s3.at[k - 1], recv_sem=r3.at[k - 1],
            device_id=plane_at(k), device_id_type=MESH)

    def give_i(k):
        return pltpu.make_async_remote_copy(
            src_ref=images.at[tower], dst_ref=images.at[tower],
            send_sem=s4.at[slot(k)], recv_sem=r4.at[slot(k)],
            device_id=tower_at(k), device_id_type=MESH)

    spread(full_t, block(plane), unit(
        flat_t, down_t, part_t, got_t, s1, r1, note_t, told_t, s7, r7))
    texts[plane, 0:rows, :] = full_t[pl.ds(block(plane), rows), :].astype(BF16)
    each(1, planes, lambda k: give_t(k).start())
    spread(full_i, block(tower), unit(
        flat_i, down_i, part_i, got_i, s2, r2, note_i, told_i, s8, r8))
    images[tower, 0:rows, :] = full_i[pl.ds(block(tower), rows), :].astype(BF16)
    line(tower, towers, lambda k: give_i(k).start())

    def take_i(k):
        give_i(k).wait_recv()
        q = partner(tower, k, towers)[1]
        full_i[pl.ds(block(q), rows), :] = images[q, 0:rows, :].astype(F32)

    def take_t(k):
        give_t(k).wait_recv()
        q = partner(plane, k, planes)[1]
        full_t[pl.ds(block(q), rows), :] = texts[q, 0:rows, :].astype(F32)

    load_scale.wait()
    load_shift.wait()
    scale = scale_ref[0]
    shift = shift_ref[0]
    cols = planes * sub
    near(1, planes, take_t)
    all_t = gather(full_t, 0, cols).astype(BF16)
    near(1, towers, take_i)
    all_i = gather(full_i, 0, group).astype(BF16)
    scores = lax.dot_general(all_i, all_t, (((1,), (1,)), ((), ())), preferred_element_type=F32)
    at_i = lax.broadcasted_iota(jnp.int32, (group, cols), 0) - tower * sub
    at_t = lax.broadcasted_iota(jnp.int32, (group, cols), 1) - plane * sub
    match = jnp.where((at_i == at_t) & (at_i >= 0) & (at_i < sub), 1.0, 0.0)
    grads = jax.nn.sigmoid(scale * scores + shift) - match

    def back_image(k):
        return pltpu.make_async_remote_copy(
            src_ref=term_i.at[partner(tower, k, towers)[0]], dst_ref=back_i.at[slot(k)],
            send_sem=s5.at[slot(k)], recv_sem=r5.at[slot(k)],
            device_id=tower_at(k), device_id_type=MESH)

    def back_text(k):
        return pltpu.make_async_remote_copy(
            src_ref=term_t.at[partner(plane, k, planes)[0]], dst_ref=back_t.at[k - 1],
            send_sem=s6.at[k - 1], recv_sem=r6.at[k - 1],
            device_id=plane_at(k), device_id_type=MESH)

    def stage(n, sums, term):
        for d in range(n):
            term[d, 0:rows, :] = sums[d * rows:(d + 1) * rows, :].astype(WIRE)

    spread(sums_i, 0, jnp.dot(grads.astype(BF16), all_t, preferred_element_type=F32))
    stage(towers, sums_i, term_i)
    line(tower, towers, lambda k: back_image(k).start())
    spread(sums_t, 0, jnp.dot(grads.T.astype(BF16), all_i, preferred_element_type=F32))
    stage(planes, sums_t, term_t)
    each(1, planes, lambda k: back_text(k).start())

    def total(sums, me, back, wait, n, out):
        near(1, n, wait)
        value = sums[pl.ds(block(me), rows), :]
        value = scale * (value + jnp.sum(back[:, 0:rows, :].astype(F32), axis=0))
        code[...] = value
        out[:, 0, :] = gather(code, 0, sub)

    total(sums_t, plane, back_t, lambda k: back_text(k).wait_recv(), planes, text_out)
    total(sums_i, tower, back_i, lambda k: back_image(k).wait_recv(), towers, image_out)

    each(1, towers, lambda k: scatter(k, note_t, told_t, s7, r7).wait_send())
    each(1, towers, lambda k: scatter(k, note_i, told_i, s8, r8).wait_send())
    each(1, towers, lambda k: scatter(k, part_t, got_t, s1, r1).wait_send())
    each(1, towers, lambda k: scatter(k, part_i, got_i, s2, r2).wait_send())
    each(1, planes, lambda k: give_t(k).wait_send())
    each(1, towers, lambda k: give_i(k).wait_send())
    each(1, towers, lambda k: back_image(k).wait_send())
    each(1, planes, lambda k: back_text(k).wait_send())


def finish(image_ref, text_ref, image_out, text_out):
    image_out[...] = image_ref[...]
    text_out[...] = text_ref[...]


def up_to(n, m):
    return -(-n // m) * m


def per_device(towers, pipes, planes, image_feats, text_tokens, lengths, w_image, w_text,
               logit_scale, logit_bias):
    group = image_feats.shape[2]
    emb = w_image.shape[1]
    sub = group // towers
    rows = sub * emb // LANES
    span = up_to(rows, 8)
    out = jax.ShapeDtypeStruct((sub, 1, emb), F32)
    sems = []
    for n in (towers, towers, planes, towers, towers, planes, towers, towers):
        sems += [pltpu.SemaphoreType.DMA((n - 1,))] * 2
    arrays = [pltpu.with_memory_space_constraint(x, pltpu.HBM) for x in (
        image_feats, text_tokens, lengths, w_image, w_text)]
    outs = pl.pallas_call(
        functools.partial(kernel, sub, towers, pipes, planes),
        out_shape=(out, out),
        in_specs=[pl.BlockSpec(memory_space=pl.ANY)] * 7,
        out_specs=(pl.BlockSpec(memory_space=pltpu.VMEM),) * 2,
        scratch_shapes=[
            pltpu.SMEM(logit_scale.shape, F32),
            pltpu.SMEM(logit_bias.shape, F32),
            pltpu.VMEM(image_feats.shape[2:], image_feats.dtype),
            pltpu.VMEM(text_tokens.shape[2:], text_tokens.dtype),
            pltpu.VMEM(lengths.shape[1:], lengths.dtype),
            pltpu.VMEM(w_image.shape, w_image.dtype),
            pltpu.VMEM(w_text.shape, w_text.dtype),
            pltpu.VMEM((towers * rows, LANES), F32),
            pltpu.VMEM((towers * rows, LANES), F32),
            pltpu.VMEM((up_to(group, 8), LANES), F32),
            pltpu.VMEM((up_to(group, 8), LANES), F32),
            pltpu.VMEM((towers, 1, LANES), F32),
            pltpu.VMEM((towers, 1, LANES), F32),
            pltpu.VMEM((towers - 1, 1, LANES), F32),
            pltpu.VMEM((towers - 1, 1, LANES), F32),
            pltpu.VMEM((towers, span, LANES), CODE),
            pltpu.VMEM((towers, span, LANES), CODE),
            pltpu.VMEM((towers - 1, span, LANES), CODE),
            pltpu.VMEM((towers - 1, span, LANES), CODE),
            pltpu.VMEM((rows, LANES), F32),
            pltpu.VMEM((towers * rows, LANES), F32),
            pltpu.VMEM((planes * rows, LANES), F32),
            pltpu.VMEM((towers, span, LANES), BF16),
            pltpu.VMEM((planes, span, LANES), BF16),
            pltpu.VMEM((towers * rows, LANES), F32),
            pltpu.VMEM((planes * rows, LANES), F32),
            pltpu.VMEM((towers, span, LANES), WIRE),
            pltpu.VMEM((planes, span, LANES), WIRE),
            pltpu.VMEM((towers - 1, span, LANES), WIRE),
            pltpu.VMEM((planes - 1, span, LANES), WIRE),
            pltpu.SemaphoreType.DMA((6 + group // (8 if group % 8 == 0 else group),)),
        ] + sems,
        compiler_params=pltpu.CompilerParams(
            collective_id=0, has_side_effects=True, vmem_limit_bytes=24 * 2**20),
    )(logit_scale, logit_bias, *arrays)
    outs = pl.pallas_call(
        finish,
        out_shape=(out, out),
        in_specs=[pl.BlockSpec(memory_space=pltpu.VMEM)] * 2,
        out_specs=(pl.BlockSpec(memory_space=pltpu.VMEM),) * 2,
        compiler_params=pltpu.CompilerParams(vmem_limit_bytes=2**20),
    )(*outs)
    return tuple(o.reshape(1, 1, sub, emb) for o in outs)


def solution(mesh):
    shape = dict(mesh.shape)
    planes = shape["loss"] * shape["pipe"]
    return jax.shard_map(
        functools.partial(per_device, shape["tower"], shape["pipe"], planes),
        mesh=mesh,
        in_specs=(
            P("loss", "pipe", None, "tower"),
            P("loss", "pipe", None, None, "tower"),
            P("loss", "pipe", None),
            P("tower", None),
            P("tower", None),
            P(),
            P(),
        ),
        out_specs=(P("loss", "pipe", "tower", None), P("loss", "pipe", "tower", None)),
        check_vma=False,
    )
```

```python
import functools

import jax
import jax.numpy as jnp
from jax import lax
from jax.experimental import pallas as pl
from jax.experimental.pallas import tpu as pltpu
from jax.sharding import PartitionSpec as P

MESH = pl.DeviceIdType.MESH
WIRE = jnp.bfloat16
CODE = jnp.int16
F32 = jnp.float32
BF16 = jnp.bfloat16
UNROLL = 16
LANES = 128
STEPS = 32752.0


def each(lo, hi, body):
    if hi - lo <= UNROLL:
        for k in reversed(range(lo, hi)):
            body(k)
    else:
        lax.fori_loop(lo, hi, lambda k, c: (body(k), c)[1], 0)


def near(lo, hi, body):
    if hi - lo <= UNROLL:
        for k in sorted(range(lo, hi), key=lambda k: (bin(k).count("1"), k)):
            body(k)
    else:
        each(lo, hi, body)


def partner(me, k, n):
    if isinstance(k, tuple):
        return k[1], k[1]
    if n <= UNROLL and n & (n - 1) == 0:
        q = me
        for b in range(n.bit_length() - 1):
            if (k >> b) & 1:
                q = q + (1 - 2 * lax.rem(me // (1 << b), 2)) * (1 << b)
        return q, q
    return lax.rem(me + k, n), lax.rem(me + n - k, n)


def slot(k):
    return (k[0] if isinstance(k, tuple) else k) - 1


def line(me, n, body):
    if n != 4:
        each(1, n, body)
        return
    upper = me // 2
    inner = lax.rem((me + 1) // 2, 2)
    body((3 - inner, 3 * (1 - upper)))
    body((2 + inner, 2 - upper))
    body(1)


def kernel(
    sub, towers, pipes, planes,
    scale_hbm, shift_hbm, feats_hbm, words_hbm, lens_hbm, wi_hbm, wt_hbm,
    image_out, text_out,
    scale_ref, shift_ref, feats, words, lens, wi, wt,
    flat_i, flat_t, down_i, down_t, note_i, note_t, told_i, told_t,
    part_i, part_t, got_i, got_t, code,
    full_i, full_t, images, texts, sums_i, sums_t, term_i, term_t, back_i, back_t,
    load_sem, s1, r1, s2, r2, s3, r3, s4, r4, s5, r5, s6, r6, s7, r7, s8, r8,
):
    group, width = feats.shape
    length = words.shape[1]
    emb = wi.shape[1]
    chunks = emb // LANES
    rows = sub * chunks
    span = term_i.shape[1]
    tower = lax.axis_index("tower")
    plane = lax.axis_index("loss") * pipes + lax.axis_index("pipe")

    def tower_at(k):
        return {"tower": partner(tower, k, towers)[0]}

    def plane_at(k):
        q = partner(plane, k, planes)[0]
        return {"loss": q // pipes, "pipe": lax.rem(q, pipes)}

    def block(i):
        at = i * rows
        return pl.multiple_of(at, 8) if rows % 8 == 0 else at

    barrier = pltpu.get_barrier_semaphore()
    each(1, towers, lambda k: pl.semaphore_signal(
        barrier, inc=1, device_id=tower_at(k), device_id_type=MESH))
    batch = 8 if group % 8 == 0 else group
    parts = group // batch
    loads = []
    for n, (src, dst) in enumerate(
        [(lens_hbm.at[0], lens)]
        + [(words_hbm.at[0, 0, c * batch:(c + 1) * batch], words.at[c * batch:(c + 1) * batch])
           for c in range(parts)]
        + [(wt_hbm, wt), (feats_hbm.at[0, 0], feats), (wi_hbm, wi),
           (scale_hbm, scale_ref), (shift_hbm, shift_ref)]
    ):
        loads.append(pltpu.make_async_copy(src, dst, load_sem.at[n]))
        loads[-1].start()
    load_lens, *load_words, load_wt, load_feats, load_wi, load_scale, load_shift = loads

    each(1, planes, lambda k: pl.semaphore_signal(
        barrier, inc=1, device_id=plane_at(k), device_id_type=MESH))

    def spread(ref, start, x):
        for c in range(chunks):
            ref[pl.ds(start + c, x.shape[0], stride=chunks), :] = x[:, c * LANES:(c + 1) * LANES]

    def gather(ref, start, n):
        return jnp.concatenate(
            [ref[pl.ds(start + c, n, stride=chunks), :] for c in range(chunks)], axis=1)

    def encode(raw, flat, down, part, note):
        most = jnp.maximum(jnp.max(jnp.abs(raw), axis=1, keepdims=True), 1e-30)
        spread(flat, 0, raw * (STEPS / most))
        step = most * (1.0 / STEPS)
        down[0:group, :] = jnp.broadcast_to(step, (group, LANES))
        row = lax.broadcasted_iota(jnp.int32, (group, LANES), 0)
        lane = lax.broadcasted_iota(jnp.int32, (group, LANES), 1)
        for d in range(towers):
            mine = (row == lane + d * sub) & (lane < sub)
            note[d] = jnp.sum(jnp.where(mine, step, 0.0), axis=0, keepdims=True)
        for d in range(towers):
            values = jnp.round(flat[d * rows:(d + 1) * rows, :])
            part[d, 0:rows, :] = values.astype(jnp.int32).astype(CODE)

    def scatter(k, part, got, send, recv):
        return pltpu.make_async_remote_copy(
            src_ref=part.at[partner(tower, k, towers)[0]], dst_ref=got.at[slot(k)],
            send_sem=send.at[slot(k)], recv_sem=recv.at[slot(k)],
            device_id=tower_at(k), device_id_type=MESH)

    load_lens.wait()
    counts = lens[...].astype(F32)
    pooled = []
    for c in range(parts):
        row = lax.broadcasted_iota(jnp.int32, (batch, group), 0) + c * batch
        mine = row == lax.broadcasted_iota(jnp.int32, (batch, group), 1)
        count = jnp.sum(jnp.where(mine, counts, 0.0), axis=1, keepdims=True)
        spot = lax.broadcasted_iota(jnp.int32, (batch, batch * length), 1)
        first = lax.broadcasted_iota(jnp.int32, (batch, batch * length), 0) * length
        keep = (spot >= first) & (spot < first + count.astype(jnp.int32))
        keep = jnp.where(keep, 1.0, 0.0).astype(BF16)
        load_words[c].wait()
        summed = jnp.dot(
            keep, words[c * batch:(c + 1) * batch].reshape(batch * length, words.shape[2]),
            preferred_element_type=F32)
        pooled.append(summed / count)
    pooled = jnp.concatenate(pooled, axis=0).astype(BF16)
    load_wt.wait()
    encode(jnp.dot(pooled, wt[...], preferred_element_type=F32), flat_t, down_t, part_t, note_t)
    pl.semaphore_wait(barrier, towers + planes - 2)
    line(tower, towers, lambda k: scatter(k, note_t, told_t, s7, r7).start())
    line(tower, towers, lambda k: scatter(k, part_t, got_t, s1, r1).start())

    load_feats.wait()
    load_wi.wait()
    encode(jnp.dot(feats[...], wi[...], preferred_element_type=F32), flat_i, down_i, part_i, note_i)
    line(tower, towers, lambda k: scatter(k, note_i, told_i, s8, r8).start())
    line(tower, towers, lambda k: scatter(k, part_i, got_i, s2, r2).start())

    def unit(flat, down, part, got, send, recv, note, told, note_send, note_recv):
        raw = gather(flat, block(tower), sub) * down[pl.ds(tower * sub, sub), 0:1]
        mine = (lax.broadcasted_iota(jnp.int32, (sub, LANES), 0)
                == lax.broadcasted_iota(jnp.int32, (sub, LANES), 1))
        for k in sorted(range(1, towers), key=lambda k: (bin(k).count("1"), k)):
            scatter(k, note, told, note_send, note_recv).wait_recv()
            step = jnp.sum(jnp.where(mine, told[k - 1], 0.0), axis=1, keepdims=True)
            scatter(k, part, got, send, recv).wait_recv()
            code[...] = got[k - 1, 0:rows, :].astype(jnp.int32).astype(F32)
            raw = raw + gather(code, 0, sub) * step
        size = jnp.sum(raw * raw, axis=-1, keepdims=True) + 1e-06
        return raw * lax.rsqrt(size)

    def give_t(k):
        return pltpu.make_async_remote_copy(
            src_ref=texts.at[plane], dst_ref=texts.at[plane],
            send_sem=s3.at[k - 1], recv_sem=r3.at[k - 1],
            device_id=plane_at(k), device_id_type=MESH)

    def give_i(k):
        return pltpu.make_async_remote_copy(
            src_ref=images.at[tower], dst_ref=images.at[tower],
            send_sem=s4.at[slot(k)], recv_sem=r4.at[slot(k)],
            device_id=tower_at(k), device_id_type=MESH)

    spread(full_t, block(plane), unit(
        flat_t, down_t, part_t, got_t, s1, r1, note_t, told_t, s7, r7))
    texts[plane, 0:rows, :] = full_t[pl.ds(block(plane), rows), :].astype(BF16)
    each(1, planes, lambda k: give_t(k).start())
    spread(full_i, block(tower), unit(
        flat_i, down_i, part_i, got_i, s2, r2, note_i, told_i, s8, r8))
    images[tower, 0:rows, :] = full_i[pl.ds(block(tower), rows), :].astype(BF16)
    line(tower, towers, lambda k: give_i(k).start())

    def take_i(k):
        give_i(k).wait_recv()
        q = partner(tower, k, towers)[1]
        full_i[pl.ds(block(q), rows), :] = images[q, 0:rows, :].astype(F32)

    def take_t(k):
        give_t(k).wait_recv()
        q = partner(plane, k, planes)[1]
        full_t[pl.ds(block(q), rows), :] = texts[q, 0:rows, :].astype(F32)

    load_scale.wait()
    load_shift.wait()
    scale = scale_ref[0]
    shift = shift_ref[0]
    cols = planes * sub
    near(1, planes, take_t)
    all_t = gather(full_t, 0, cols).astype(BF16)
    near(1, towers, take_i)
    all_i = gather(full_i, 0, group).astype(BF16)
    scores = lax.dot_general(all_i, all_t, (((1,), (1,)), ((), ())), preferred_element_type=F32)
    at_i = lax.broadcasted_iota(jnp.int32, (group, cols), 0) - tower * sub
    at_t = lax.broadcasted_iota(jnp.int32, (group, cols), 1) - plane * sub
    match = jnp.where((at_i == at_t) & (at_i >= 0) & (at_i < sub), 1.0, 0.0)
    grads = jax.nn.sigmoid(scale * scores + shift) - match

    def back_image(k):
        return pltpu.make_async_remote_copy(
            src_ref=term_i.at[partner(tower, k, towers)[0]], dst_ref=back_i.at[slot(k)],
            send_sem=s5.at[slot(k)], recv_sem=r5.at[slot(k)],
            device_id=tower_at(k), device_id_type=MESH)

    def back_text(k):
        return pltpu.make_async_remote_copy(
            src_ref=term_t.at[partner(plane, k, planes)[0]], dst_ref=back_t.at[k - 1],
            send_sem=s6.at[k - 1], recv_sem=r6.at[k - 1],
            device_id=plane_at(k), device_id_type=MESH)

    def stage(q, sums, term):
        term[q, 0:rows, :] = sums[pl.ds(block(q), rows), :].astype(WIRE)

    def return_image(k):
        stage(partner(tower, k, towers)[0], sums_i, term_i)
        back_image(k).start()

    def return_text(k):
        stage(partner(plane, k, planes)[0], sums_t, term_t)
        back_text(k).start()

    spread(sums_i, 0, jnp.dot(grads.astype(BF16), all_t, preferred_element_type=F32))
    line(tower, towers, return_image)
    spread(sums_t, 0, jnp.dot(grads.T.astype(BF16), all_i, preferred_element_type=F32))
    each(1, planes, return_text)

    def total(sums, me, back, wait, n, out):
        near(1, n, wait)
        value = sums[pl.ds(block(me), rows), :]
        value = scale * (value + jnp.sum(back[:, 0:rows, :].astype(F32), axis=0))
        code[...] = value
        out[:, 0, :] = gather(code, 0, sub)

    total(sums_t, plane, back_t, lambda k: back_text(k).wait_recv(), planes, text_out)
    total(sums_i, tower, back_i, lambda k: back_image(k).wait_recv(), towers, image_out)

    each(1, towers, lambda k: scatter(k, note_t, told_t, s7, r7).wait_send())
    each(1, towers, lambda k: scatter(k, note_i, told_i, s8, r8).wait_send())
    each(1, towers, lambda k: scatter(k, part_t, got_t, s1, r1).wait_send())
    each(1, towers, lambda k: scatter(k, part_i, got_i, s2, r2).wait_send())
    each(1, planes, lambda k: give_t(k).wait_send())
    each(1, towers, lambda k: give_i(k).wait_send())
    each(1, towers, lambda k: back_image(k).wait_send())
    each(1, planes, lambda k: back_text(k).wait_send())


def finish(image_ref, text_ref, image_out, text_out):
    image_out[...] = image_ref[...]
    text_out[...] = text_ref[...]


def up_to(n, m):
    return -(-n // m) * m


def per_device(towers, pipes, planes, image_feats, text_tokens, lengths, w_image, w_text,
               logit_scale, logit_bias):
    group = image_feats.shape[2]
    emb = w_image.shape[1]
    sub = group // towers
    rows = sub * emb // LANES
    span = up_to(rows, 8)
    out = jax.ShapeDtypeStruct((sub, 1, emb), F32)
    sems = []
    for n in (towers, towers, planes, towers, towers, planes, towers, towers):
        sems += [pltpu.SemaphoreType.DMA((n - 1,))] * 2
    arrays = [pltpu.with_memory_space_constraint(x, pltpu.HBM) for x in (
        image_feats, text_tokens, lengths, w_image, w_text)]
    outs = pl.pallas_call(
        functools.partial(kernel, sub, towers, pipes, planes),
        out_shape=(out, out),
        in_specs=[pl.BlockSpec(memory_space=pl.ANY)] * 7,
        out_specs=(pl.BlockSpec(memory_space=pltpu.VMEM),) * 2,
        scratch_shapes=[
            pltpu.SMEM(logit_scale.shape, F32),
            pltpu.SMEM(logit_bias.shape, F32),
            pltpu.VMEM(image_feats.shape[2:], image_feats.dtype),
            pltpu.VMEM(text_tokens.shape[2:], text_tokens.dtype),
            pltpu.VMEM(lengths.shape[1:], lengths.dtype),
            pltpu.VMEM(w_image.shape, w_image.dtype),
            pltpu.VMEM(w_text.shape, w_text.dtype),
            pltpu.VMEM((towers * rows, LANES), F32),
            pltpu.VMEM((towers * rows, LANES), F32),
            pltpu.VMEM((up_to(group, 8), LANES), F32),
            pltpu.VMEM((up_to(group, 8), LANES), F32),
            pltpu.VMEM((towers, 1, LANES), F32),
            pltpu.VMEM((towers, 1, LANES), F32),
            pltpu.VMEM((towers - 1, 1, LANES), F32),
            pltpu.VMEM((towers - 1, 1, LANES), F32),
            pltpu.VMEM((towers, span, LANES), CODE),
            pltpu.VMEM((towers, span, LANES), CODE),
            pltpu.VMEM((towers - 1, span, LANES), CODE),
            pltpu.VMEM((towers - 1, span, LANES), CODE),
            pltpu.VMEM((rows, LANES), F32),
            pltpu.VMEM((towers * rows, LANES), F32),
            pltpu.VMEM((planes * rows, LANES), F32),
            pltpu.VMEM((towers, span, LANES), BF16),
            pltpu.VMEM((planes, span, LANES), BF16),
            pltpu.VMEM((towers * rows, LANES), F32),
            pltpu.VMEM((planes * rows, LANES), F32),
            pltpu.VMEM((towers, span, LANES), WIRE),
            pltpu.VMEM((planes, span, LANES), WIRE),
            pltpu.VMEM((towers - 1, span, LANES), WIRE),
            pltpu.VMEM((planes - 1, span, LANES), WIRE),
            pltpu.SemaphoreType.DMA((6 + group // (8 if group % 8 == 0 else group),)),
        ] + sems,
        compiler_params=pltpu.CompilerParams(
            collective_id=0, has_side_effects=True, vmem_limit_bytes=24 * 2**20),
    )(logit_scale, logit_bias, *arrays)
    outs = pl.pallas_call(
        finish,
        out_shape=(out, out),
        in_specs=[pl.BlockSpec(memory_space=pltpu.VMEM)] * 2,
        out_specs=(pl.BlockSpec(memory_space=pltpu.VMEM),) * 2,
        compiler_params=pltpu.CompilerParams(vmem_limit_bytes=2**20),
    )(*outs)
    return tuple(o.reshape(1, 1, sub, emb) for o in outs)


def solution(mesh):
    shape = dict(mesh.shape)
    planes = shape["loss"] * shape["pipe"]
    return jax.shard_map(
        functools.partial(per_device, shape["tower"], shape["pipe"], planes),
        mesh=mesh,
        in_specs=(
            P("loss", "pipe", None, "tower"),
            P("loss", "pipe", None, None, "tower"),
            P("loss", "pipe", None),
            P("tower", None),
            P("tower", None),
            P(),
            P(),
        ),
        out_specs=(P("loss", "pipe", "tower", None), P("loss", "pipe", "tower", None)),
        check_vma=False,
    )
```

```python
import functools

import jax
import jax.numpy as jnp
from jax import lax
from jax.experimental import pallas as pl
from jax.experimental.pallas import tpu as pltpu
from jax.sharding import PartitionSpec as P

MESH = pl.DeviceIdType.MESH
WIRE = jnp.bfloat16
CODE = jnp.int16
F32 = jnp.float32
BF16 = jnp.bfloat16
UNROLL = 16
LANES = 128
STEPS = 32752.0


def each(lo, hi, body):
    if hi - lo <= UNROLL:
        for k in reversed(range(lo, hi)):
            body(k)
    else:
        lax.fori_loop(lo, hi, lambda k, c: (body(k), c)[1], 0)


def near(lo, hi, body):
    if hi - lo <= UNROLL:
        for k in sorted(range(lo, hi), key=lambda k: (bin(k).count("1"), k)):
            body(k)
    else:
        each(lo, hi, body)


def far(lo, hi, step, body):
    if hi - lo <= UNROLL:
        for k in sorted(range(lo, hi), key=lambda k: (-bin(k & ~step).count("1"), -k)):
            body(k)
    else:
        each(lo, hi, body)


def partner(me, k, n):
    if isinstance(k, tuple):
        return k[1], k[1]
    if n <= UNROLL and n & (n - 1) == 0:
        q = me
        for b in range(n.bit_length() - 1):
            if (k >> b) & 1:
                q = q + (1 - 2 * lax.rem(me // (1 << b), 2)) * (1 << b)
        return q, q
    return lax.rem(me + k, n), lax.rem(me + n - k, n)


def slot(k):
    return (k[0] if isinstance(k, tuple) else k) - 1


def line(me, n, body):
    if n != 4:
        each(1, n, body)
        return
    upper = me // 2
    inner = lax.rem((me + 1) // 2, 2)
    body((3 - inner, 3 * (1 - upper)))
    body((2 + inner, 2 - upper))
    body(1)


def kernel(
    sub, towers, pipes, planes,
    scale_hbm, shift_hbm, feats_hbm, words_hbm, lens_hbm, wi_hbm, wt_hbm,
    image_out, text_out,
    scale_ref, shift_ref, feats, words, lens, wi, wt,
    flat_i, flat_t, down_i, down_t, note_i, note_t, told_i, told_t,
    part_i, part_t, got_i, got_t, code,
    full_i, full_t, images, texts, sums_i, sums_t, term_i, term_t, back_i, back_t,
    load_sem, s1, r1, s2, r2, s3, r3, s4, r4, s5, r5, s6, r6, s7, r7, s8, r8,
):
    group, width = feats.shape
    length = words.shape[1]
    emb = wi.shape[1]
    chunks = emb // LANES
    rows = sub * chunks
    span = term_i.shape[1]
    tower = lax.axis_index("tower")
    plane = lax.axis_index("loss") * pipes + lax.axis_index("pipe")

    def tower_at(k):
        return {"tower": partner(tower, k, towers)[0]}

    def plane_at(k):
        q = partner(plane, k, planes)[0]
        return {"loss": q // pipes, "pipe": lax.rem(q, pipes)}

    def block(i):
        at = i * rows
        return pl.multiple_of(at, 8) if rows % 8 == 0 else at

    barrier = pltpu.get_barrier_semaphore()
    each(1, towers, lambda k: pl.semaphore_signal(
        barrier, inc=1, device_id=tower_at(k), device_id_type=MESH))
    batch = 8 if group % 8 == 0 else group
    parts = group // batch
    loads = []
    for n, (src, dst) in enumerate(
        [(lens_hbm.at[0], lens)]
        + [(words_hbm.at[0, 0, c * batch:(c + 1) * batch], words.at[c * batch:(c + 1) * batch])
           for c in range(parts)]
        + [(wt_hbm, wt), (feats_hbm.at[0, 0], feats), (wi_hbm, wi),
           (scale_hbm, scale_ref), (shift_hbm, shift_ref)]
    ):
        loads.append(pltpu.make_async_copy(src, dst, load_sem.at[n]))
        loads[-1].start()
    load_lens, *load_words, load_wt, load_feats, load_wi, load_scale, load_shift = loads

    each(1, planes, lambda k: pl.semaphore_signal(
        barrier, inc=1, device_id=plane_at(k), device_id_type=MESH))

    def spread(ref, start, x):
        for c in range(chunks):
            ref[pl.ds(start + c, x.shape[0], stride=chunks), :] = x[:, c * LANES:(c + 1) * LANES]

    def gather(ref, start, n):
        return jnp.concatenate(
            [ref[pl.ds(start + c, n, stride=chunks), :] for c in range(chunks)], axis=1)

    def encode(raw, flat, down, part, note):
        most = jnp.maximum(jnp.max(jnp.abs(raw), axis=1, keepdims=True), 1e-30)
        spread(flat, 0, raw * (STEPS / most))
        step = most * (1.0 / STEPS)
        down[0:group, :] = jnp.broadcast_to(step, (group, LANES))
        row = lax.broadcasted_iota(jnp.int32, (group, LANES), 0)
        lane = lax.broadcasted_iota(jnp.int32, (group, LANES), 1)
        for d in range(towers):
            mine = (row == lane + d * sub) & (lane < sub)
            note[d] = jnp.sum(jnp.where(mine, step, 0.0), axis=0, keepdims=True)
        for d in range(towers):
            values = jnp.round(flat[d * rows:(d + 1) * rows, :])
            part[d, 0:rows, :] = values.astype(jnp.int32).astype(CODE)

    def scatter(k, part, got, send, recv):
        return pltpu.make_async_remote_copy(
            src_ref=part.at[partner(tower, k, towers)[0]], dst_ref=got.at[slot(k)],
            send_sem=send.at[slot(k)], recv_sem=recv.at[slot(k)],
            device_id=tower_at(k), device_id_type=MESH)

    load_lens.wait()
    counts = lens[...].astype(F32)
    pooled = []
    for c in range(parts):
        row = lax.broadcasted_iota(jnp.int32, (batch, group), 0) + c * batch
        mine = row == lax.broadcasted_iota(jnp.int32, (batch, group), 1)
        count = jnp.sum(jnp.where(mine, counts, 0.0), axis=1, keepdims=True)
        spot = lax.broadcasted_iota(jnp.int32, (batch, batch * length), 1)
        first = lax.broadcasted_iota(jnp.int32, (batch, batch * length), 0) * length
        keep = (spot >= first) & (spot < first + count.astype(jnp.int32))
        keep = jnp.where(keep, 1.0, 0.0).astype(BF16)
        load_words[c].wait()
        summed = jnp.dot(
            keep, words[c * batch:(c + 1) * batch].reshape(batch * length, words.shape[2]),
            preferred_element_type=F32)
        pooled.append(summed / count)
    pooled = jnp.concatenate(pooled, axis=0).astype(BF16)
    load_wt.wait()
    encode(jnp.dot(pooled, wt[...], preferred_element_type=F32), flat_t, down_t, part_t, note_t)
    pl.semaphore_wait(barrier, towers + planes - 2)
    line(tower, towers, lambda k: scatter(k, note_t, told_t, s7, r7).start())
    line(tower, towers, lambda k: scatter(k, part_t, got_t, s1, r1).start())

    load_feats.wait()
    load_wi.wait()
    encode(jnp.dot(feats[...], wi[...], preferred_element_type=F32), flat_i, down_i, part_i, note_i)
    line(tower, towers, lambda k: scatter(k, note_i, told_i, s8, r8).start())
    line(tower, towers, lambda k: scatter(k, part_i, got_i, s2, r2).start())

    def unit(flat, down, part, got, send, recv, note, told, note_send, note_recv):
        raw = gather(flat, block(tower), sub) * down[pl.ds(tower * sub, sub), 0:1]
        mine = (lax.broadcasted_iota(jnp.int32, (sub, LANES), 0)
                == lax.broadcasted_iota(jnp.int32, (sub, LANES), 1))
        for k in sorted(range(1, towers), key=lambda k: (bin(k).count("1"), k)):
            scatter(k, note, told, note_send, note_recv).wait_recv()
            step = jnp.sum(jnp.where(mine, told[k - 1], 0.0), axis=1, keepdims=True)
            scatter(k, part, got, send, recv).wait_recv()
            code[...] = got[k - 1, 0:rows, :].astype(jnp.int32).astype(F32)
            raw = raw + gather(code, 0, sub) * step
        size = jnp.sum(raw * raw, axis=-1, keepdims=True) + 1e-06
        return raw * lax.rsqrt(size)

    def give_t(k):
        return pltpu.make_async_remote_copy(
            src_ref=texts.at[plane], dst_ref=texts.at[plane],
            send_sem=s3.at[k - 1], recv_sem=r3.at[k - 1],
            device_id=plane_at(k), device_id_type=MESH)

    def give_i(k):
        return pltpu.make_async_remote_copy(
            src_ref=images.at[tower], dst_ref=images.at[tower],
            send_sem=s4.at[slot(k)], recv_sem=r4.at[slot(k)],
            device_id=tower_at(k), device_id_type=MESH)

    spread(full_t, block(plane), unit(
        flat_t, down_t, part_t, got_t, s1, r1, note_t, told_t, s7, r7))
    texts[plane, 0:rows, :] = full_t[pl.ds(block(plane), rows), :].astype(BF16)
    far(1, planes, pipes, lambda k: give_t(k).start())
    spread(full_i, block(tower), unit(
        flat_i, down_i, part_i, got_i, s2, r2, note_i, told_i, s8, r8))
    images[tower, 0:rows, :] = full_i[pl.ds(block(tower), rows), :].astype(BF16)
    line(tower, towers, lambda k: give_i(k).start())

    def take_i(k):
        give_i(k).wait_recv()
        q = partner(tower, k, towers)[1]
        full_i[pl.ds(block(q), rows), :] = images[q, 0:rows, :].astype(F32)

    def take_t(k):
        give_t(k).wait_recv()
        q = partner(plane, k, planes)[1]
        full_t[pl.ds(block(q), rows), :] = texts[q, 0:rows, :].astype(F32)

    load_scale.wait()
    load_shift.wait()
    scale = scale_ref[0]
    shift = shift_ref[0]
    cols = planes * sub
    near(1, planes, take_t)
    all_t = gather(full_t, 0, cols).astype(BF16)
    near(1, towers, take_i)
    all_i = gather(full_i, 0, group).astype(BF16)
    scores = lax.dot_general(all_i, all_t, (((1,), (1,)), ((), ())), preferred_element_type=F32)
    at_i = lax.broadcasted_iota(jnp.int32, (group, cols), 0) - tower * sub
    at_t = lax.broadcasted_iota(jnp.int32, (group, cols), 1) - plane * sub
    match = jnp.where((at_i == at_t) & (at_i >= 0) & (at_i < sub), 1.0, 0.0)
    grads = jax.nn.sigmoid(scale * scores + shift) - match

    def back_image(k):
        return pltpu.make_async_remote_copy(
            src_ref=term_i.at[partner(tower, k, towers)[0]], dst_ref=back_i.at[slot(k)],
            send_sem=s5.at[slot(k)], recv_sem=r5.at[slot(k)],
            device_id=tower_at(k), device_id_type=MESH)

    def back_text(k):
        return pltpu.make_async_remote_copy(
            src_ref=term_t.at[partner(plane, k, planes)[0]], dst_ref=back_t.at[k - 1],
            send_sem=s6.at[k - 1], recv_sem=r6.at[k - 1],
            device_id=plane_at(k), device_id_type=MESH)

    def stage(n, sums, term):
        for d in range(n):
            term[d, 0:rows, :] = sums[d * rows:(d + 1) * rows, :].astype(WIRE)

    spread(sums_i, 0, jnp.dot(grads.astype(BF16), all_t, preferred_element_type=F32))
    stage(towers, sums_i, term_i)
    line(tower, towers, lambda k: back_image(k).start())
    spread(sums_t, 0, jnp.dot(grads.T.astype(BF16), all_i, preferred_element_type=F32))
    stage(planes, sums_t, term_t)
    far(1, planes, pipes, lambda k: back_text(k).start())

    def total(sums, me, back, wait, n, out):
        near(1, n, wait)
        value = sums[pl.ds(block(me), rows), :]
        value = scale * (value + jnp.sum(back[:, 0:rows, :].astype(F32), axis=0))
        code[...] = value
        out[:, 0, :] = gather(code, 0, sub)

    total(sums_t, plane, back_t, lambda k: back_text(k).wait_recv(), planes, text_out)
    total(sums_i, tower, back_i, lambda k: back_image(k).wait_recv(), towers, image_out)

    each(1, towers, lambda k: scatter(k, note_t, told_t, s7, r7).wait_send())
    each(1, towers, lambda k: scatter(k, note_i, told_i, s8, r8).wait_send())
    each(1, towers, lambda k: scatter(k, part_t, got_t, s1, r1).wait_send())
    each(1, towers, lambda k: scatter(k, part_i, got_i, s2, r2).wait_send())
    each(1, planes, lambda k: give_t(k).wait_send())
    each(1, towers, lambda k: give_i(k).wait_send())
    each(1, towers, lambda k: back_image(k).wait_send())
    each(1, planes, lambda k: back_text(k).wait_send())


def finish(image_ref, text_ref, image_out, text_out):
    image_out[...] = image_ref[...]
    text_out[...] = text_ref[...]


def up_to(n, m):
    return -(-n // m) * m


def per_device(towers, pipes, planes, image_feats, text_tokens, lengths, w_image, w_text,
               logit_scale, logit_bias):
    group = image_feats.shape[2]
    emb = w_image.shape[1]
    sub = group // towers
    rows = sub * emb // LANES
    span = up_to(rows, 8)
    out = jax.ShapeDtypeStruct((sub, 1, emb), F32)
    sems = []
    for n in (towers, towers, planes, towers, towers, planes, towers, towers):
        sems += [pltpu.SemaphoreType.DMA((n - 1,))] * 2
    arrays = [pltpu.with_memory_space_constraint(x, pltpu.HBM) for x in (
        image_feats, text_tokens, lengths, w_image, w_text)]
    outs = pl.pallas_call(
        functools.partial(kernel, sub, towers, pipes, planes),
        out_shape=(out, out),
        in_specs=[pl.BlockSpec(memory_space=pl.ANY)] * 7,
        out_specs=(pl.BlockSpec(memory_space=pltpu.VMEM),) * 2,
        scratch_shapes=[
            pltpu.SMEM(logit_scale.shape, F32),
            pltpu.SMEM(logit_bias.shape, F32),
            pltpu.VMEM(image_feats.shape[2:], image_feats.dtype),
            pltpu.VMEM(text_tokens.shape[2:], text_tokens.dtype),
            pltpu.VMEM(lengths.shape[1:], lengths.dtype),
            pltpu.VMEM(w_image.shape, w_image.dtype),
            pltpu.VMEM(w_text.shape, w_text.dtype),
            pltpu.VMEM((towers * rows, LANES), F32),
            pltpu.VMEM((towers * rows, LANES), F32),
            pltpu.VMEM((up_to(group, 8), LANES), F32),
            pltpu.VMEM((up_to(group, 8), LANES), F32),
            pltpu.VMEM((towers, 1, LANES), F32),
            pltpu.VMEM((towers, 1, LANES), F32),
            pltpu.VMEM((towers - 1, 1, LANES), F32),
            pltpu.VMEM((towers - 1, 1, LANES), F32),
            pltpu.VMEM((towers, span, LANES), CODE),
            pltpu.VMEM((towers, span, LANES), CODE),
            pltpu.VMEM((towers - 1, span, LANES), CODE),
            pltpu.VMEM((towers - 1, span, LANES), CODE),
            pltpu.VMEM((rows, LANES), F32),
            pltpu.VMEM((towers * rows, LANES), F32),
            pltpu.VMEM((planes * rows, LANES), F32),
            pltpu.VMEM((towers, span, LANES), BF16),
            pltpu.VMEM((planes, span, LANES), BF16),
            pltpu.VMEM((towers * rows, LANES), F32),
            pltpu.VMEM((planes * rows, LANES), F32),
            pltpu.VMEM((towers, span, LANES), WIRE),
            pltpu.VMEM((planes, span, LANES), WIRE),
            pltpu.VMEM((towers - 1, span, LANES), WIRE),
            pltpu.VMEM((planes - 1, span, LANES), WIRE),
            pltpu.SemaphoreType.DMA((6 + group // (8 if group % 8 == 0 else group),)),
        ] + sems,
        compiler_params=pltpu.CompilerParams(
            collective_id=0, has_side_effects=True, vmem_limit_bytes=24 * 2**20),
    )(logit_scale, logit_bias, *arrays)
    outs = pl.pallas_call(
        finish,
        out_shape=(out, out),
        in_specs=[pl.BlockSpec(memory_space=pltpu.VMEM)] * 2,
        out_specs=(pl.BlockSpec(memory_space=pltpu.VMEM),) * 2,
        compiler_params=pltpu.CompilerParams(vmem_limit_bytes=2**20),
    )(*outs)
    return tuple(o.reshape(1, 1, sub, emb) for o in outs)


def solution(mesh):
    shape = dict(mesh.shape)
    planes = shape["loss"] * shape["pipe"]
    return jax.shard_map(
        functools.partial(per_device, shape["tower"], shape["pipe"], planes),
        mesh=mesh,
        in_specs=(
            P("loss", "pipe", None, "tower"),
            P("loss", "pipe", None, None, "tower"),
            P("loss", "pipe", None),
            P("tower", None),
            P("tower", None),
            P(),
            P(),
        ),
        out_specs=(P("loss", "pipe", "tower", None), P("loss", "pipe", "tower", None)),
        check_vma=False,
    )
```
